256 devices in a mesh: vol: 32 (over z, y), rep: 8 (over x, core).
Axes of the slice: x: 4, y: 4, z: 8, core: 2. Of those that a mesh axis runs over, the one named last changes fastest.
Arguments:
- features: bfloat16 [32, 32, 4, 16384], P('vol', None, None, 'rep'), may hold values from -6 to 6
- deltas: float32 [32, 4, 16384], P('vol', None, 'rep'), may hold values from 0.003125 to 0.03125
- counts: int32 [32, 16384], P('vol', 'rep'), may hold values from 0 to 4
- order_rank: int32 [16384, 32], P('rep'), may hold values from 0 to 31, each once within a row
- cotangent: float32 [3, 16384], P(None, 'rep'), may hold values from -6 to 6
- first_weight: bfloat16 [32, 32, 256], P('vol'), may hold values from -1.5 to 1.5
- middle_weight: bfloat16 [32, 2, 256, 256], P('vol'), may hold values from -0.5 to 0.5
- last_weight: bfloat16 [32, 256, 4], P('vol'), may hold values from -0.375 to 0.375
Outputs:
- first_grad: float32 [32, 32, 256], P('vol')
- middle_grad: float32 [32, 2, 256, 256], P('vol')
- last_grad: float32 [32, 256, 4], P('vol')
The draws below stay inside these ranges and needn't reach their ends.
Inputs may be any that keep to these rules, and one draw needn't show every extreme that they name: `order_rank`: each ray's row holds every number of 0 .. 31 once.
All inputs are finite; a program needn't handle non-finite values.
Results may differ from the reference program's by a relative error of at most 0.0083.
Values sent between devices are 32-bit elements; how exact they have to be, the bound alone decides.
No kernel may reach another device: no remote copies, remote signals or barrier semaphores. Data moves between devices by JAX's collectives and lax.ppermute only.
A program may use at most 128 MiB of HBM per device.

```python
import math
import jax
import jax.numpy as jnp
from jax import lax

FEAT = 32
W = 256
HID = 2
SAMP = 4
NV = 32
NR = 16384


def touch_ends(array, stream_key, least, largest):
    longest = array.shape.index(max(array.shape))
    spots = []
    for shift in (0, 1):
        where = [jax.random.randint(jax.random.fold_in(stream_key, axis), (), 0, length) for axis, length in enumerate(array.shape)]
        where[longest] = (where[longest] + shift) % array.shape[longest]
        spots.append(tuple(where))
    return array.at[spots[0]].set(least).at[spots[1]].set(largest)


def levels(own_key, dims, pieces, low, top_value):
    level = 1.0
    for axis_at, shards_of in pieces:
        steps = jax.random.uniform(jax.random.fold_in(jax.random.fold_in(own_key, 6), axis_at), (shards_of,), jnp.float32, low / len(pieces), top_value / len(pieces))
        level = level * jnp.repeat(jnp.exp(steps), dims[axis_at] // shards_of).reshape((-1,) + (1,) * (len(dims) - 1 - axis_at))
    return level


def gaussian(key, extent, width, reach, shards=(), kind=jnp.bfloat16):
    gain = levels(key, extent, shards, -0.22, 0.18) if shards else 1.0
    result = jax.random.normal(key, extent, jnp.float32) * width * gain
    return jnp.minimum(jnp.maximum(result, -reach), reach).astype(kind)


def setup_inputs(seed: int = 0) -> dict:
    streams_of = jax.random.split(jax.random.key(seed), 9)
    return {
        "features": gaussian(streams_of[0], (NV, FEAT, SAMP, NR), 1.0, 6.0, ((0, 32), (3, 8))),
        "deltas": jnp.clip(jnp.exp(math.log(0.03125) - 2.3025851 * jax.random.uniform(streams_of[1], (NV, SAMP, NR), jnp.float32) ** levels(streams_of[1], (NV, SAMP, NR), ((0, 32), (2, 8)), -0.2, 0.2)), 0.003125, 0.03125),
        "counts": touch_ends(jax.random.randint(streams_of[2], (NV, NR), 0, SAMP + 1), jax.random.fold_in(streams_of[2], 1), 0, SAMP).astype(jnp.int32),
        "order_rank": jax.vmap(lambda own: jax.random.permutation(own, NV))(jax.random.split(streams_of[3], NR)).reshape((NR, NV)).astype(jnp.int32),
        "cotangent": gaussian(streams_of[4], (3, NR), 1.0, 6.0, ((1, 8),), jnp.float32),
        "first_weight": gaussian(streams_of[5], (NV, FEAT, W), (FEAT // 2) ** -0.5, 1.5, ((0, 32),)),
        "middle_weight": gaussian(streams_of[6], (NV, HID, W, W), (W // 2) ** -0.5, 0.5, ((0, 32),)),
        "last_weight": gaussian(streams_of[7], (NV, W, 4), W ** -0.5, 0.375, ((0, 32),)),
    }


def contract_first(matrix, rows):
    return lax.dot_general(matrix, rows, (((0,), (0,)), ((), ())), preferred_element_type=jnp.float32)

def contract_last(left, right):
    return lax.dot_general(left, right, (((1,), (1,)), ((), ())), preferred_element_type=jnp.float32)

def silu_grad(pre):
    logistic = jax.nn.sigmoid(pre)
    return logistic * (1.0 + pre * (1.0 - logistic))

def forward_network(samples, first_weight, middle_weight, last_weight):
    pre = contract_first(first_weight, samples)
    preacts = [pre]
    layer_inputs = [samples]
    hidden = jax.nn.silu(pre).astype(jnp.bfloat16)
    for depth in range(middle_weight.shape[0]):
        layer_inputs.append(hidden)
        pre = contract_first(middle_weight[depth], hidden)
        preacts.append(pre)
        hidden = jax.nn.silu(pre).astype(jnp.bfloat16)
    layer_inputs.append(hidden)
    head_out = contract_first(last_weight, hidden)
    return (preacts, layer_inputs, head_out)

def render_segment(head_out, deltas, counts):
    density = jax.nn.softplus(head_out[0])
    albedo = jax.nn.sigmoid(head_out[1:])
    live = (lax.broadcasted_iota(jnp.int32, deltas.shape, 0) < counts[None, :]).astype(jnp.float32)
    optical = density * deltas * live
    reached = jnp.cumsum(optical, axis=0)
    passed = reached - optical
    leaving = jnp.exp(-reached)
    sample_weight = jnp.exp(-passed) - leaving
    colour = lax.optimization_barrier(jnp.sum(sample_weight[None] * albedo, axis=1))
    logt = -reached[-1]
    return (colour, logt, (albedo, leaving, sample_weight, live))

def head_gradient(head_out, deltas, saved, grad_colour, grad_logt):
    albedo, leaving, sample_weight, live = saved
    facing = lax.optimization_barrier(jnp.sum(grad_colour[:, None, :] * albedo, axis=0))
    weighted = facing * sample_weight
    later = lax.optimization_barrier(jnp.sum(weighted, axis=0))[None] - jnp.cumsum(weighted, axis=0)
    doptical = facing * leaving - later - grad_logt[None]
    d_density = doptical * deltas * live * jax.nn.sigmoid(head_out[0])
    d_albedo = sample_weight[None] * grad_colour[:, None, :] * albedo * (1.0 - albedo)
    return jnp.concatenate([d_density[None], d_albedo], axis=0).astype(jnp.bfloat16)

def network_gradients(preacts, layer_inputs, head_grad, middle_weight, last_weight, reducers):
    last_grad = reducers[0](contract_last(layer_inputs[-1], head_grad))
    back = (jnp.dot(last_weight, head_grad, preferred_element_type=jnp.float32) * silu_grad(preacts[-1])).astype(jnp.bfloat16)
    hidden_grads = []
    for depth in reversed(range(middle_weight.shape[0])):
        hidden_grads.append(reducers[1](contract_last(layer_inputs[depth + 1], back)))
        back = (jnp.dot(middle_weight[depth], back, preferred_element_type=jnp.float32) * silu_grad(preacts[depth])).astype(jnp.bfloat16)
    first_grad = reducers[2](contract_last(layer_inputs[0], back))
    middle_grad = jnp.stack(hidden_grads[::-1], axis=0)
    return (first_grad, middle_grad, last_grad)

def composite_rays(segments, rank_rows, cotangent):
    logs = segments[:, 3]

    def add_log(index, total):
        other = lax.dynamic_index_in_dim(rank_rows, index, 0, keepdims=True)
        term = lax.dynamic_index_in_dim(logs, index, 0, keepdims=True)
        return total + jnp.where(other < rank_rows, term, 0.0)
    summed = lax.fori_loop(0, rank_rows.shape[0], add_log, jnp.zeros(rank_rows.shape, jnp.float32))
    prefix = jnp.exp(summed)
    facing = lax.optimization_barrier(jnp.sum(cotangent[None] * segments[:, :3], axis=1)) * prefix

    def add_behind(index, total):
        other = lax.dynamic_index_in_dim(rank_rows, index, 0, keepdims=True)
        term = lax.dynamic_index_in_dim(facing, index, 0, keepdims=True)
        return total + jnp.where(other > rank_rows, term, 0.0)
    behind = lax.fori_loop(0, rank_rows.shape[0], add_behind, jnp.zeros(rank_rows.shape, jnp.float32))
    return (prefix, behind)

def unchanged(value):
    return value

def reference(features, deltas, counts, order_rank, cotangent, first_weight, middle_weight, last_weight):

    def forward_one(bundle):
        feat_block, delta_block, count_block, weight_one, weight_two, weight_three = bundle
        samples = feat_block.reshape(feat_block.shape[0], -1)
        preacts, layer_inputs, head_out = forward_network(samples, weight_one, weight_two, weight_three)
        shaped = head_out.reshape(4, delta_block.shape[0], delta_block.shape[1])
        colour, logt, saved = render_segment(shaped, delta_block, count_block)
        return jnp.concatenate([colour, logt[None]], axis=0)
    segments = lax.map(forward_one, (features, deltas, counts, first_weight, middle_weight, last_weight))
    prefix, behind = composite_rays(segments, order_rank.T, cotangent)

    def backward_one(bundle):
        feat_block, delta_block, count_block, weight_one, weight_two, weight_three, own_prefix, own_behind = bundle
        samples = feat_block.reshape(feat_block.shape[0], -1)
        preacts, layer_inputs, head_out = forward_network(samples, weight_one, weight_two, weight_three)
        shaped = head_out.reshape(4, delta_block.shape[0], delta_block.shape[1])
        colour, logt, saved = render_segment(shaped, delta_block, count_block)
        grad_colour = own_prefix[None] * cotangent
        head_grad = head_gradient(shaped, delta_block, saved, grad_colour, own_behind).reshape(4, -1)
        return network_gradients(preacts, layer_inputs, head_grad, weight_two, weight_three, (unchanged, unchanged, unchanged))
    first_grad, middle_grad, last_grad = lax.map(backward_one, (features, deltas, counts, first_weight, middle_weight, last_weight, prefix, behind))
    return (first_grad, middle_grad, last_grad)
```

```python
import functools

import jax
import jax.numpy as jnp
from jax import lax
from jax.experimental import pallas as pl
from jax.experimental.pallas import tpu as pltpu
from jax.sharding import Mesh, PartitionSpec as P

F32 = jnp.float32
BF16 = jnp.bfloat16
CHUNKS = 2
TILE = 256
SAMP = 4
FEAT = 32
W = 256
NV = 32


def dot(lhs, rhs, lhs_dim, rhs_dim, precision=None):
    return lax.dot_general(
        lhs, rhs, (((lhs_dim,), (rhs_dim,)), ((), ())),
        preferred_element_type=F32, precision=precision,
    )


def group_rows(rows, width):
    i = lax.broadcasted_iota(jnp.int32, (rows, width), 0)
    j = lax.broadcasted_iota(jnp.int32, (rows, width), 1)
    return lax.shift_right_logical(i, 2) == j


def spread(block, fill):
    row = lax.broadcasted_iota(jnp.int32, block.shape, 0)
    parts = [jnp.where((row & 3) == s, block, fill) for s in range(SAMP)]
    return jnp.concatenate(parts, axis=1)


def lane_rows(value):
    return [value[:, 128 * i : 128 * (i + 1)] for i in range(value.shape[1] // 128)]


def forward_kernel(
    x_ref, delta_ref, count_ref, cot_ref, w1_ref, wm_ref, w4_ref,
    save_ref, ab_ref, pay_ref, w1t, wmt, w4t, rows,
):
    step = pl.program_id(0)
    tile = x_ref.shape[1]

    @pl.when(step == 0)
    def _():
        pick = group_rows(FEAT * SAMP, FEAT).astype(BF16)
        w1t[...] = (dot(w1_ref[...], pick, 0, 1) * 0.5).astype(BF16)
        for k in range(2):
            wmt[k] = (wm_ref[k].astype(F32).T * 0.5).astype(BF16)
        pick4 = group_rows(4 * SAMP, 4).astype(BF16)
        w4t[...] = dot(pick4, w4_ref[...], 1, 1).astype(BF16)

    wide = spread(x_ref[...], jnp.zeros((), BF16))
    half = dot(w1t[...], wide, 1, 0)
    for k in range(3):
        bent = 1.0 + jnp.tanh(half)
        hid = half * bent
        slope = bent + hid * (2.0 - bent)
        hidden = hid.astype(BF16)
        save_ref[k] = hidden
        save_ref[3 + k] = slope.astype(BF16)
        if k < 2:
            half = dot(wmt[k], hidden, 1, 0)
    row16 = lax.broadcasted_iota(jnp.int32, (4 * SAMP, W), 0) & 3
    head = jnp.zeros((4 * SAMP, tile), F32)
    for s in range(SAMP):
        head += dot(
            jnp.where(row16 == s, w4t[...], jnp.zeros((), BF16)),
            hidden[:, s * tile : (s + 1) * tile], 1, 0,
        )

    logistic = jax.nn.sigmoid(head)
    density = jnp.maximum(head[:4], 0.0) + jnp.log1p(jnp.exp(-jnp.abs(head[:4])))
    live = lax.broadcasted_iota(jnp.int32, (SAMP, tile), 0) < count_ref[...]
    span = jnp.where(live, delta_ref[...], 0.0)
    optical = density * span
    sums = [optical[0:1]]
    for s in range(1, SAMP):
        sums.append(sums[-1] + optical[s : s + 1])
    reached = jnp.concatenate(sums, axis=0)
    leaving = jnp.exp(-reached)
    entering = jnp.concatenate([jnp.ones((1, tile), F32), leaving[:3]], axis=0)
    share = entering - leaving
    cot = cot_ref[...]
    parts = []
    facing = jnp.zeros((SAMP, tile), F32)
    for c in range(3):
        albedo = logistic[4 * (c + 1) : 4 * (c + 2)]
        lit = cot[c : c + 1] * albedo
        facing += lit
        parts.append(share * lit * (1.0 - albedo))
    weighted = facing * share
    total = weighted[3:4]
    later = [jnp.zeros((1, tile), F32), total]
    for s in (2, 1):
        total = total + weighted[s : s + 1]
        later.append(total)
    whole = total + weighted[0:1]
    later = jnp.concatenate(later[::-1], axis=0)
    own = span * logistic[:4]
    ab_ref[...] = jnp.concatenate(
        [(facing * leaving - later) * own] + parts + [own, jnp.zeros((4, tile), F32)], axis=0
    )
    per = tile // 128
    for i, (a, b) in enumerate(zip(lane_rows(-sums[-1]), lane_rows(whole))):
        rows[pl.ds(step * per + i, 1), :] = a
        rows[pl.ds(8 + step * per + i, 1), :] = b

    @pl.when(step == pl.num_programs(0) - 1)
    def _():
        pay_ref[...] = jnp.broadcast_to(rows[...][None], pay_ref.shape)


def backward_kernel(last, first, *refs):
    refs = list(refs)
    place_ref = refs.pop(0)
    save_ref, ab_ref, x_ref, got_ref, rank_ref, wm_ref, w4_ref = refs[:7]
    refs = refs[7:]
    if not first:
        before = refs[:3]
        refs = refs[3:]
    if last:
        keep_ref, send_ref = refs[:2]
        refs = refs[2:]
        front, own, mids, firsts, lasts = refs
    else:
        mids, firsts, lasts, front, own = refs
    step = pl.program_id(0)
    tile = x_ref.shape[1]

    @pl.when(step == 0)
    def _():
        if first:
            mids[...] = jnp.zeros_like(mids)
            firsts[...] = jnp.zeros_like(firsts)
            lasts[...] = jnp.zeros_like(lasts)
        else:
            mids[...] = before[0][...]
            firsts[...] = before[1][...]
            lasts[...] = before[2][...]

        def one(v, _):
            mine = rank_ref[v]
            total = jnp.zeros((8, 128), F32)
            for u in range(NV):
                total += jnp.where(rank_ref[u] < mine, got_ref[u, :8], 0.0)
            front[v] = jnp.exp(total)
            return 0

        lax.fori_loop(0, NV, one, 0)
        me = place_ref[0]
        mine = rank_ref[me]
        behind = jnp.zeros((8, 128), F32)
        for u in range(NV):
            behind += jnp.where(rank_ref[u] > mine, front[u] * got_ref[u, 8:], 0.0)
        own[:8] = front[me]
        own[8:] = behind

    per = tile // 128
    prefix = jnp.concatenate([own[pl.ds(step * per + i, 1), :] for i in range(per)], axis=1)
    behind = jnp.concatenate([own[pl.ds(8 + step * per + i, 1), :] for i in range(per)], axis=1)
    ghead = ab_ref[:16] * prefix
    ghead = jnp.concatenate([ghead[:4] - ab_ref[16:20] * behind, ghead[4:]], axis=0)
    ghead = spread(ghead.astype(BF16), jnp.zeros((), BF16))

    pick4 = (group_rows(4 * SAMP, 4).astype(F32) * 0.5).astype(BF16)
    lasts[...] += dot(save_ref[2], ghead, 1, 1)
    back = dot(dot(w4_ref[...], pick4, 1, 1).astype(BF16), ghead, 1, 0)
    back = (back * save_ref[5].astype(F32)).astype(BF16)
    for k in (1, 0):
        mids[k] += dot(save_ref[k], back, 1, 1)
        halved = (wm_ref[k].astype(F32) * 0.5).astype(BF16)
        back = (dot(halved, back, 1, 0) * save_ref[3 + k].astype(F32)).astype(BF16)
    firsts[...] += dot(spread(x_ref[...], jnp.zeros((), BF16)), back, 1, 1)

    if last:

        @pl.when(step == pl.num_programs(0) - 1)
        def _():
            highest = lax.Precision.HIGHEST
            pick = group_rows(FEAT * SAMP, FEAT).astype(F32)
            small = dot(pick, firsts[...], 0, 0, highest)
            pick8 = group_rows(4 * SAMP, 8).astype(F32)
            tail = dot(pick8, lasts[...], 0, 1, highest)
            for side in range(2):
                cols = slice(128 * side, 128 * (side + 1))

                def fill(ref):
                    ref[0:256, :] = mids[1][:, cols]
                    ref[256:512, :] = mids[0][:, cols]
                    ref[512:544, :] = small[:, cols]
                    ref[544:552, :] = tail[:, cols]

                @pl.when(place_ref[1] == side)
                def _():
                    fill(keep_ref)

                @pl.when(place_ref[1] != side)
                def _():
                    fill(send_ref)


def unpack_kernel(place_ref, mine_ref, other_ref, first_ref, mid_ref, last_ref):
    for side in range(2):
        cols = slice(128 * side, 128 * (side + 1))

        def emit(ref):
            mid_ref[1, :, cols] = ref[0:256, :]
            mid_ref[0, :, cols] = ref[256:512, :]
            first_ref[:, cols] = ref[512:544, :]
            last_ref[cols, :] = ref[544:552, :].T[:, :4]

        @pl.when(place_ref[0] == side)
        def _():
            emit(mine_ref)

        @pl.when(place_ref[0] != side)
        def _():
            emit(other_ref)


LIMIT = 48 * 1024 * 1024


def forward(chunk, x, deltas, counts, cot, w1, wm, w4):
    rays = x.shape[1] // CHUNKS
    steps = rays // TILE
    at = chunk * steps
    whole2 = lambda i: (0, 0)
    return pl.pallas_call(
        forward_kernel,
        grid=(steps,),
        in_specs=[
            pl.BlockSpec((FEAT * SAMP, TILE), lambda i: (0, at + i)),
            pl.BlockSpec((SAMP, TILE), lambda i: (0, at + i)),
            pl.BlockSpec((1, TILE), lambda i: (0, at + i)),
            pl.BlockSpec((3, TILE), lambda i: (0, at + i)),
            pl.BlockSpec((FEAT, W), whole2),
            pl.BlockSpec((2, W, W), lambda i: (0, 0, 0)),
            pl.BlockSpec((W, 4), whole2),
        ],
        out_specs=[
            pl.BlockSpec((6, W, SAMP * TILE), lambda i: (0, 0, i)),
            pl.BlockSpec((24, TILE), lambda i: (0, i)),
            pl.BlockSpec((NV, 16, 128), lambda i: (0, 0, 0)),
        ],
        out_shape=[
            jax.ShapeDtypeStruct((6, W, SAMP * rays), BF16),
            jax.ShapeDtypeStruct((24, rays), F32),
            jax.ShapeDtypeStruct((NV, 16, 128), F32),
        ],
        scratch_shapes=[
            pltpu.VMEM((W, FEAT * SAMP), BF16),
            pltpu.VMEM((2, W, W), BF16),
            pltpu.VMEM((4 * SAMP, W), BF16),
            pltpu.VMEM((16, 128), F32),
        ],
        compiler_params=pltpu.CompilerParams(vmem_limit_bytes=LIMIT),
        cost_estimate=pl.CostEstimate(
            flops=2 * SAMP * rays * 140288, transcendentals=3 * W * SAMP * rays,
            bytes_accessed=13 * 2**20,
        ),
        name=f"forward{chunk}",
    )(x, deltas, counts, cot, w1, wm, w4)


def backward(chunk, place, saved, x, got, ranks, wm, w4, before):
    save, ab = saved
    rays = ab.shape[1]
    steps = rays // TILE
    at = chunk * steps
    first, last = chunk == 0, chunk == CHUNKS - 1
    sums = [
        ((2, W, W), F32),
        ((FEAT * SAMP, W), F32),
        ((W, 4 * SAMP), F32),
    ]
    const = lambda nd: (lambda i, p: (0,) * nd)
    sum_specs = [pl.BlockSpec(shape, const(len(shape))) for shape, _ in sums]
    in_specs = [
        pl.BlockSpec((6, W, SAMP * TILE), lambda i, p: (0, 0, i)),
        pl.BlockSpec((24, TILE), lambda i, p: (0, i)),
        pl.BlockSpec((FEAT * SAMP, TILE), lambda i, p: (0, at + i)),
        pl.BlockSpec((NV, 16, 128), const(3)),
        pl.BlockSpec((NV, 8, 128), lambda i, p: (0, chunk, 0)),
        pl.BlockSpec((2, W, W), const(3)),
        pl.BlockSpec((W, 4), const(2)),
    ]
    scratch = [pltpu.VMEM((NV, 8, 128), F32), pltpu.VMEM((16, 128), F32)]
    if not first:
        in_specs += sum_specs
    if last:
        out_specs = [pl.BlockSpec((552, 128), const(2))] * 2
        out_shape = [jax.ShapeDtypeStruct((552, 128), F32)] * 2
        scratch += [pltpu.VMEM(shape, kind) for shape, kind in sums]
    else:
        out_specs = sum_specs
        out_shape = [jax.ShapeDtypeStruct(shape, kind) for shape, kind in sums]
    return pl.pallas_call(
        functools.partial(backward_kernel, last, first),
        grid_spec=pltpu.PrefetchScalarGridSpec(
            num_scalar_prefetch=1, grid=(steps,), in_specs=in_specs, out_specs=out_specs,
            scratch_shapes=scratch,
        ),
        out_shape=out_shape,
        compiler_params=pltpu.CompilerParams(vmem_limit_bytes=LIMIT),
        cost_estimate=pl.CostEstimate(
            flops=2 * SAMP * rays * 280000, transcendentals=0, bytes_accessed=13 * 2**20
        ),
        name=f"backward{chunk}",
    )(place, save, ab, x, got, ranks, wm, w4, *before)


PAIR = [(0, 1), (1, 0)]
NEAR = [(0, 1), (1, 0), (2, 3), (3, 2)]
FAR = [(0, 3), (3, 0), (1, 2), (2, 1)]


def per_device(
    features, deltas, counts, order_rank, cotangent, first_weight, middle_weight, last_weight
):
    x = features[0].reshape(FEAT * SAMP, -1)
    core = lax.axis_index("core")
    place = jnp.stack([lax.axis_index(("z", "y")), core]).astype(jnp.int32)
    ranks = order_rank.T.reshape(NV, -1, 128)
    w1, wm, w4 = first_weight[0], middle_weight[0], last_weight[0]
    saved, got = [], []
    for chunk in range(CHUNKS):
        save, ab, pay = forward(chunk, x, deltas[0], counts, cotangent, w1, wm, w4)
        saved.append((save, ab))
        got.append(lax.all_to_all(pay, ("z", "y"), 0, 0, tiled=True))
    sums = ()
    for chunk in range(CHUNKS):
        sums = backward(chunk, place, saved[chunk], x, got[chunk], ranks, wm, w4, sums)
    keep, send = sums
    keep = keep + lax.ppermute(send, "core", PAIR)
    a, b = keep[:280], keep[280:]
    a, b = a + lax.ppermute(a, "x", NEAR), b + lax.ppermute(b, "x", FAR)
    a, b = a + lax.ppermute(a, "x", FAR), b + lax.ppermute(b, "x", NEAR)
    mine = jnp.concatenate([a, b], axis=0)
    other = lax.ppermute(mine, "core", PAIR)
    first, mid, tail = pl.pallas_call(
        unpack_kernel,
        grid_spec=pltpu.PrefetchScalarGridSpec(
            num_scalar_prefetch=1, grid=(1,),
            in_specs=[pl.BlockSpec((552, 128), lambda i, p: (0, 0))] * 2,
            out_specs=[
                pl.BlockSpec((FEAT, W), lambda i, p: (0, 0)),
                pl.BlockSpec((2, W, W), lambda i, p: (0, 0, 0)),
                pl.BlockSpec((W, 4), lambda i, p: (0, 0)),
            ],
        ),
        out_shape=[
            jax.ShapeDtypeStruct((FEAT, W), F32),
            jax.ShapeDtypeStruct((2, W, W), F32),
            jax.ShapeDtypeStruct((W, 4), F32),
        ],
        name="unpack",
    )(core.reshape(1).astype(jnp.int32), mine, other)
    return (first[None], mid[None], tail[None])


def solution(mesh):
    fine = Mesh(mesh.devices.reshape(8, 4, 4, 2), ("z", "y", "x", "core"))
    vol, rep = ("z", "y"), ("x", "core")
    placed = (
        P(vol, None, None, rep),
        P(vol, None, rep),
        P(vol, rep),
        P(rep, None),
        P(None, rep),
        P(vol, None, None),
        P(vol, None, None, None),
        P(vol, None, None),
    )
    return jax.shard_map(
        per_device,
        mesh=fine,
        in_specs=placed,
        out_specs=(P(vol, None, None), P(vol, None, None, None), P(vol, None, None)),
        check_vma=False,
    )
```

```python
import jax
import jax.numpy as jnp
from jax import lax
from jax.experimental import pallas as pl
from jax.experimental.pallas import tpu as pltpu
from jax.sharding import Mesh, PartitionSpec as P


F32 = jnp.float32
BF16 = jnp.bfloat16
TILE = 512
SAMP = 4
FEAT = 32
W = 256
NV = 32
MIB = 1024 * 1024
HBM = pltpu.MemorySpace.HBM
VMEM = pltpu.MemorySpace.VMEM
SMEM = pltpu.MemorySpace.SMEM
LIMIT = 24 * MIB


def dot(lhs, rhs, lhs_dim, rhs_dim, precision=None):
    return lax.dot_general(
        lhs, rhs, (((lhs_dim,), (rhs_dim,)), ((), ())),
        preferred_element_type=F32, precision=precision,
    )


def group_rows(rows, width):
    i = lax.broadcasted_iota(jnp.int32, (rows, width), 0)
    j = lax.broadcasted_iota(jnp.int32, (rows, width), 1)
    return lax.shift_right_logical(i, 2) == j


def spread(block, fill):
    row = lax.broadcasted_iota(jnp.int32, block.shape, 0)
    parts = [jnp.where((row & 3) == s, block, fill) for s in range(SAMP)]
    return jnp.concatenate(parts, axis=1)


def by_row(ref, row):
    planes, rows, _ = ref.shape
    return ref.reshape(planes * rows, 128)[pl.ds(row, planes, stride=rows), :]


def forward_kernel(
    x_ref, delta_ref, count_ref, cot_ref, w1_ref, wm_ref, w4_ref,
    deep_ref, low_ref, half_ref, ab_ref, pay_ref, w1t, wmt, w4t, heads, given,
):
    step = pl.program_id(0)
    tile = TILE

    @pl.when(step == 0)
    def _():
        pick = group_rows(FEAT * SAMP, FEAT).astype(BF16)
        w1t[...] = (dot(w1_ref[...], pick, 0, 1) * 0.5).astype(BF16)
        for k in range(2):
            wmt[k] = (wm_ref[k].astype(F32).T * 0.5).astype(BF16)
        pick4 = group_rows(4 * SAMP, 4).astype(BF16)
        w4t[...] = dot(pick4, w4_ref[...], 1, 0).astype(BF16)
        for r in range(given.shape[0]):
            lanes = slice(128 * r, 128 * (r + 1))
            given[r, 0:4, :] = delta_ref[:, lanes]
            given[r, 4:5, :] = count_ref[:, lanes].astype(F32)
            given[r, 5:8, :] = cot_ref[:, lanes]

    rays = pl.ds(pl.multiple_of(step * tile, tile), tile)
    wide = spread(x_ref[:, rays], jnp.zeros((), BF16))
    half = dot(w1t[...], wide, 1, 0)
    for k in range(3):
        curve = jnp.tanh(half)
        value = half + half * curve
        hidden = value.astype(BF16)
        if k == 0:
            low_ref[0] = hidden
        else:
            deep_ref[0, k - 1] = hidden
        if k < 2:
            half_ref[0, k] = half.astype(BF16)
            half = dot(wmt[k], hidden, 1, 0)
        else:
            deep_ref[0, 2] = ((1.0 + curve) + value * (1.0 - curve)).astype(BF16)
    row16 = lax.broadcasted_iota(jnp.int32, (4 * SAMP, W), 0) & 3
    head = jnp.zeros((4 * SAMP, tile), F32)
    for s in range(SAMP):
        head += dot(
            jnp.where(row16 == s, w4t[...], jnp.zeros((), BF16)),
            hidden[:, s * tile : (s + 1) * tile], 1, 0,
        )
    for r in range(tile // 128):
        heads[step * (tile // 128) + r] = head[:, 128 * r : 128 * (r + 1)]

    @pl.when(step == pl.num_programs(0) - 1)
    def _():
        render(heads, given, ab_ref, pay_ref)


def render(heads, given, ab_ref, pay_ref):
    planes = heads.shape[0]
    zero = jnp.zeros((planes, 128), F32)
    counts = by_row(given, 4)
    cot = [by_row(given, 5 + c) for c in range(3)]
    reached, leaving = zero, jnp.ones((planes, 128), F32)
    share, left, facing, own = [], [], [], []
    for s in range(SAMP):
        raw = by_row(heads, s)
        density = jnp.maximum(raw, 0.0) + jnp.log1p(jnp.exp(-jnp.abs(raw)))
        span = jnp.where(counts > s, by_row(given, s), 0.0)
        reached = reached + density * span
        entering, leaving = leaving, jnp.exp(-reached)
        share.append(entering - leaving)
        left.append(leaving)
        own.append(span * jax.nn.sigmoid(raw))
        total = zero
        for c in range(3):
            albedo = jax.nn.sigmoid(by_row(heads, 4 * (c + 1) + s))
            lit = cot[c] * albedo
            total = total + lit
            ab_ref[4 * (c + 1) + s] = share[s] * lit * (1.0 - albedo)
        facing.append(total)
    later = zero
    for s in reversed(range(SAMP)):
        ab_ref[s] = (facing[s] * left[s] - later) * own[s]
        ab_ref[16 + s] = own[s]
        later = later + facing[s] * share[s]
    both = jnp.concatenate([-reached, later], axis=0)
    pay_ref[...] = jnp.broadcast_to(both[None], pay_ref.shape)


def slope_kernel(half_ref, low_ref, mid_ref):
    for k, ref in enumerate((low_ref, mid_ref)):
        for at in range(0, W, 64):
            half = half_ref[0, k, at : at + 64, :].astype(F32)
            curve = jnp.tanh(half)
            value = half * curve
            ref[0, at : at + 64, :] = ((1.0 + half) + curve * (1.0 - value)).astype(BF16)


def split(place_ref, keep_ref, send_ref, pieces):
    for side in range(2):
        cols = slice(128 * side, 128 * (side + 1))

        def fill(ref):
            at = 0
            for piece in pieces:
                ref[at : at + piece.shape[0], :] = piece[:, cols]
                at += piece.shape[0]

        @pl.when(place_ref[1] == side)
        def _():
            fill(keep_ref)

        @pl.when(place_ref[1] != side)
        def _():
            fill(send_ref)


def top_kernel(
    place_ref, deep_hbm, ab_ref, got_ref, rank_ref, w4_ref,
    back_ref, keep_ref, send_ref, deep, front, heads, mid, last, w4h, sems,
):
    steps = deep.shape[0]
    for i in range(steps):
        pltpu.make_async_copy(deep_hbm.at[i], deep.at[i], sems.at[i]).start()

    planes = rank_ref.shape[1]

    def one(v, _):
        mine = rank_ref[v]
        total = jnp.zeros((planes, 128), F32)
        for u in range(NV):
            total += jnp.where(rank_ref[u] < mine, got_ref[u, :planes], 0.0)
        front[v] = jnp.exp(total)
        return 0

    lax.fori_loop(0, NV, one, 0)
    me = place_ref[0]
    mine = rank_ref[me]
    behind = jnp.zeros((planes, 128), F32)
    for u in range(NV):
        behind += jnp.where(rank_ref[u] > mine, front[u] * got_ref[u, planes:], 0.0)
    prefix = front[me]
    rows = heads.reshape(planes * 4 * SAMP, 128)
    for r in range(4 * SAMP):
        value = ab_ref[r] * prefix
        if r < SAMP:
            value = value - ab_ref[16 + r] * behind
        rows[pl.ds(r, planes, stride=4 * SAMP), :] = value
    mid[...] = jnp.zeros_like(mid)
    last[...] = jnp.zeros_like(last)
    pick4 = (group_rows(4 * SAMP, 4).astype(F32) * 0.5).astype(BF16)
    w4h[...] = dot(w4_ref[...], pick4, 0, 1).astype(BF16)
    per = TILE // 128

    def step(i, _):
        pltpu.make_async_copy(deep_hbm.at[i], deep.at[i], sems.at[i]).wait()
        ghead = jnp.concatenate([heads[i * per + j] for j in range(per)], axis=1)
        ghead = spread(ghead.astype(BF16), jnp.zeros((), BF16))
        back = dot(w4h[...], ghead, 1, 0)
        back = (back * deep[i, 2].astype(F32)).astype(BF16)
        back_ref[i] = back
        last[...] += dot(deep[i, 1], ghead, 1, 1)
        mid[...] += dot(deep[i, 0], back, 1, 1)
        return 0

    lax.fori_loop(0, steps, step, 0)
    pick8 = group_rows(4 * SAMP, 8).astype(F32)
    tail = dot(pick8, last[...], 0, 1, lax.Precision.HIGHEST)
    split(place_ref, keep_ref, send_ref, (mid[...], tail))


def middle_kernel(
    place_ref, hid_ref, slope_ref, back_ref, wm_ref, down_ref, keep_ref, send_ref, mid, halved
):
    mid[...] = jnp.zeros_like(mid)
    halved[...] = (wm_ref[1].astype(F32) * 0.5).astype(BF16)

    def step(i, _):
        down = dot(halved[...], back_ref[i], 1, 0)
        down = (down * slope_ref[i].astype(F32)).astype(BF16)
        down_ref[i] = down
        mid[...] += dot(hid_ref[i], down, 1, 1)
        return 0

    lax.fori_loop(0, hid_ref.shape[0], step, 0)
    split(place_ref, keep_ref, send_ref, (mid[...],))


def low_kernel(
    place_ref, slope_ref, x_ref, back_ref, wm_ref, keep_ref, send_ref, first, halved
):
    first[...] = jnp.zeros_like(first)
    halved[...] = (wm_ref[0].astype(F32) * 0.5).astype(BF16)

    def step(i, _):
        rays = pl.ds(pl.multiple_of(i * TILE, TILE), TILE)
        down = dot(halved[...], back_ref[i], 1, 0)
        down = (down * slope_ref[i].astype(F32)).astype(BF16)
        first[...] += dot(spread(x_ref[:, rays], jnp.zeros((), BF16)), down, 1, 1)
        return 0

    lax.fori_loop(0, slope_ref.shape[0], step, 0)
    pick = group_rows(FEAT * SAMP, FEAT).astype(F32)
    small = dot(pick, first[...], 0, 0, lax.Precision.HIGHEST)
    split(place_ref, keep_ref, send_ref, (small,))


def unpack_kernel(place_ref, a_ref, a_other, b_ref, b_other, first_ref, mid_ref, last_ref):
    for side in range(2):
        cols = slice(128 * side, 128 * (side + 1))

        def emit(up, down):
            mid_ref[1, :, cols] = up[0:256, :]
            last_ref[:, cols] = up[256:260, :]
            mid_ref[0, :, cols] = down[0:256, :]
            first_ref[:, cols] = down[256:288, :]

        @pl.when(place_ref[1] == side)
        def _():
            emit(a_ref, b_ref)

        @pl.when(place_ref[1] != side)
        def _():
            emit(a_other, b_other)


def far(value):
    return pltpu.with_memory_space_constraint(value, HBM)


def near(value):
    return pltpu.with_memory_space_constraint(value, VMEM)


def forward(x, deltas, counts, cot, w1, wm, w4):
    rays = x.shape[1]
    whole2 = lambda i: (0, 0)
    inside = pl.BlockSpec(memory_space=VMEM)
    return pl.pallas_call(
        forward_kernel,
        grid=(rays // TILE,),
        in_specs=[
            inside,
            pl.BlockSpec((SAMP, rays), whole2),
            pl.BlockSpec((1, rays), whole2),
            pl.BlockSpec((3, rays), whole2),
            pl.BlockSpec((FEAT, W), whole2),
            pl.BlockSpec((2, W, W), lambda i: (0, 0, 0)),
            pl.BlockSpec((4, W), whole2),
        ],
        out_specs=[
            pl.BlockSpec((1, 3, W, SAMP * TILE), lambda i: (i, 0, 0, 0)),
            pl.BlockSpec((1, W, SAMP * TILE), lambda i: (i, 0, 0)),
            pl.BlockSpec((1, 2, W, SAMP * TILE), lambda i: (i, 0, 0, 0)),
        ] + [inside] * 2,
        out_shape=[
            pltpu.HBM((rays // TILE, 3, W, SAMP * TILE), BF16),
            pltpu.HBM((rays // TILE, W, SAMP * TILE), BF16),
            pltpu.HBM((rays // TILE, 2, W, SAMP * TILE), BF16),
            pltpu.VMEM((20, rays // 128, 128), F32),
            pltpu.VMEM((NV, 2 * rays // 128, 128), F32),
        ],
        scratch_shapes=[
            pltpu.VMEM((W, FEAT * SAMP), BF16),
            pltpu.VMEM((2, W, W), BF16),
            pltpu.VMEM((4 * SAMP, W), BF16),
            pltpu.VMEM((rays // 128, 4 * SAMP, 128), F32),
            pltpu.VMEM((rays // 128, 8, 128), F32),
        ],
        compiler_params=pltpu.CompilerParams(vmem_limit_bytes=40 * MIB),
        cost_estimate=pl.CostEstimate(
            flops=2 * SAMP * rays * 140288, transcendentals=3 * W * SAMP * rays,
            bytes_accessed=MIB,
        ),
        name="forward",
    )(near(x), far(deltas), far(counts), far(cot), far(w1), far(wm), far(w4))


def slopes(half):
    steps, _, _, n = half.shape
    block = pl.BlockSpec((1, W, n), lambda i: (i, 0, 0))
    return pl.pallas_call(
        slope_kernel,
        grid=(steps,),
        in_specs=[pl.BlockSpec((1, 2, W, n), lambda i: (i, 0, 0, 0))],
        out_specs=[block] * 2,
        out_shape=[pltpu.HBM((steps, W, n), BF16)] * 2,
        compiler_params=pltpu.CompilerParams(vmem_limit_bytes=LIMIT),
        cost_estimate=pl.CostEstimate(
            flops=6 * half.size, transcendentals=half.size, bytes_accessed=16 * MIB
        ),
        name="slopes",
    )(far(half))


def top(place, deep, ab, got, ranks, w4):
    inside = pl.BlockSpec(memory_space=VMEM)
    steps, _, _, n = deep.shape
    return pl.pallas_call(
        top_kernel,
        in_specs=[pl.BlockSpec(memory_space=SMEM), pl.BlockSpec(memory_space=HBM)] + [inside] * 4,
        out_specs=[inside] * 3,
        out_shape=[
            pltpu.VMEM((steps, W, n), BF16),
            pltpu.VMEM((264, 128), F32),
            pltpu.VMEM((264, 128), F32),
        ],
        scratch_shapes=[
            pltpu.VMEM(deep.shape, BF16),
            pltpu.VMEM((NV,) + ab.shape[1:], F32),
            pltpu.VMEM((ab.shape[1], 4 * SAMP, 128), F32),
            pltpu.VMEM((W, W), F32),
            pltpu.VMEM((W, 4 * SAMP), F32),
            pltpu.VMEM((W, 4 * SAMP), BF16),
            pltpu.SemaphoreType.DMA((steps,)),
        ],
        compiler_params=pltpu.CompilerParams(vmem_limit_bytes=24 * MIB),
        cost_estimate=pl.CostEstimate(
            flops=2 * steps * n * 80000, transcendentals=0, bytes_accessed=12 * MIB
        ),
        name="top",
    )(place, far(deep), near(ab), near(got), near(ranks), near(w4))


def middle(place, hid, slope, back, wm):
    inside = pl.BlockSpec(memory_space=VMEM)
    steps, _, n = hid.shape
    return pl.pallas_call(
        middle_kernel,
        in_specs=[pl.BlockSpec(memory_space=SMEM)] + [inside] * 4,
        out_specs=[inside] * 3,
        out_shape=[
            pltpu.VMEM((steps, W, n), BF16),
            pltpu.VMEM((256, 128), F32),
            pltpu.VMEM((256, 128), F32),
        ],
        scratch_shapes=[pltpu.VMEM((W, W), F32), pltpu.VMEM((W, W), BF16)],
        compiler_params=pltpu.CompilerParams(vmem_limit_bytes=12 * MIB),
        cost_estimate=pl.CostEstimate(
            flops=2 * steps * n * 131072, transcendentals=0, bytes_accessed=8 * MIB
        ),
        name="middle",
    )(place, near(hid), near(slope), near(back), near(wm))


def low(place, slope, x, back, wm):
    inside = pl.BlockSpec(memory_space=VMEM)
    steps, _, n = slope.shape
    return pl.pallas_call(
        low_kernel,
        in_specs=[pl.BlockSpec(memory_space=SMEM)] + [inside] * 4,
        out_specs=[inside] * 2,
        out_shape=[pltpu.VMEM((32, 128), F32), pltpu.VMEM((32, 128), F32)],
        scratch_shapes=[pltpu.VMEM((FEAT * SAMP, W), F32), pltpu.VMEM((W, W), BF16)],
        compiler_params=pltpu.CompilerParams(vmem_limit_bytes=12 * MIB),
        cost_estimate=pl.CostEstimate(
            flops=2 * steps * n * 90000, transcendentals=0, bytes_accessed=8 * MIB
        ),
        name="low",
    )(place, near(slope), near(x), near(back), near(wm))


def unpack(place, a, a_other, b, b_other):
    inside = pl.BlockSpec(memory_space=VMEM)
    return pl.pallas_call(
        unpack_kernel,
        grid=(1,),
        in_specs=[pl.BlockSpec(memory_space=pltpu.MemorySpace.SMEM)] + [inside] * 4,
        out_specs=[
            pl.BlockSpec((FEAT, W), lambda i: (0, 0)),
            pl.BlockSpec((2, W, W), lambda i: (0, 0, 0)),
            pl.BlockSpec((4, W), lambda i: (0, 0)),
        ],
        out_shape=[
            pltpu.HBM((FEAT, W), F32),
            pltpu.HBM((2, W, W), F32),
            pltpu.HBM((4, W), F32),
        ],
        compiler_params=pltpu.CompilerParams(vmem_limit_bytes=12 * MIB),
        name="unpack",
    )(place, near(a), near(a_other), near(b), near(b_other))


PAIR = [(0, 1), (1, 0)]
NEAR = [(0, 1), (1, 0), (2, 3), (3, 2)]
FAR = [(0, 3), (3, 0), (1, 2), (2, 1)]


def over_cores(keep, send):
    got = lax.ppermute(send, "core", PAIR)
    return keep + got


def over_x(value, ring):
    got = lax.ppermute(value, "x", ring)
    return value + got


def per_device(
    features, deltas, counts, order_rank, cotangent, first_weight, middle_weight, last_weight
):
    x = features[0].reshape(FEAT * SAMP, -1)
    place = jnp.stack([lax.axis_index(("z", "y")), lax.axis_index("core")]).astype(jnp.int32)
    ranks = order_rank.T.reshape(NV, -1, 128)
    w1, wm, w4 = first_weight[0], middle_weight[0], last_weight[0].T
    deep, hid, half, ab, pay = forward(x, deltas[0], counts, cotangent, w1, wm, w4)
    got = lax.all_to_all(pay, ("z", "y"), 0, 0, tiled=True)
    low_slope, mid_slope = slopes(half)
    back, *sums = top(place, deep, ab, got, ranks, w4)
    upper = over_cores(*sums)
    back, *sums = middle(place, hid, mid_slope, back, wm)
    upper = over_x(upper, NEAR)
    lower = over_cores(*sums)
    sums = low(place, low_slope, x, back, wm)
    upper = over_x(upper, FAR)
    lower = jnp.concatenate([lower, over_cores(*sums)], axis=0)
    lower = over_x(over_x(lower, NEAR), FAR)
    other = lax.ppermute(upper, "core", PAIR), lax.ppermute(lower, "core", PAIR)
    first, mid, last = unpack(place, upper, other[0], lower, other[1])
    return (first[None], mid[None], last.T[None])


def solution(mesh):
    fine = Mesh(mesh.devices.reshape(8, 4, 4, 2), ("z", "y", "x", "core"))
    vol, rep = ("z", "y"), ("x", "core")
    placed = (
        P(vol, None, None, rep),
        P(vol, None, rep),
        P(vol, rep),
        P(rep, None),
        P(None, rep),
        P(vol, None, None),
        P(vol, None, None, None),
        P(vol, None, None),
    )
    return jax.shard_map(
        per_device,
        mesh=fine,
        in_specs=placed,
        out_specs=(P(vol, None, None), P(vol, None, None, None), P(vol, None, None)),
        check_vma=False,
    )
```

```python
import jax
import jax.numpy as jnp
from jax import lax
from jax.experimental import pallas as pl
from jax.experimental.pallas import tpu as pltpu
from jax.sharding import Mesh, PartitionSpec as P


F32 = jnp.float32
BF16 = jnp.bfloat16
TILE = 512
PART = 256
SAMP = 4
FEAT = 32
W = 256
NV = 32
MIB = 1024 * 1024
HBM = pltpu.MemorySpace.HBM
VMEM = pltpu.MemorySpace.VMEM
SMEM = pltpu.MemorySpace.SMEM
LIMIT = 24 * MIB


def dot(lhs, rhs, lhs_dim, rhs_dim, precision=None):
    return lax.dot_general(
        lhs, rhs, (((lhs_dim,), (rhs_dim,)), ((), ())),
        preferred_element_type=F32, precision=precision,
    )


def group_rows(rows, width):
    i = lax.broadcasted_iota(jnp.int32, (rows, width), 0)
    j = lax.broadcasted_iota(jnp.int32, (rows, width), 1)
    return lax.shift_right_logical(i, 2) == j


def spread(block, fill):
    row = lax.broadcasted_iota(jnp.int32, block.shape, 0)
    parts = [jnp.where((row & 3) == s, block, fill) for s in range(SAMP)]
    return jnp.concatenate(parts, axis=1)


def by_row(ref, row):
    planes, rows, _ = ref.shape
    return ref.reshape(planes * rows, 128)[pl.ds(row, planes, stride=rows), :]


def forward_kernel(
    x_ref, delta_ref, count_ref, cot_ref, w1_ref, wm_ref, w4_ref,
    hid_ref, low_ref, ab_ref, pay_ref, w1t, wmt, w4t, heads, given,
):
    step = pl.program_id(0)
    tile = TILE

    @pl.when(step == 0)
    def _():
        pick = group_rows(FEAT * SAMP, FEAT).astype(BF16)
        w1t[...] = (dot(w1_ref[...], pick, 0, 1) * 0.5).astype(BF16)
        for k in range(2):
            wmt[k] = (wm_ref[k].astype(F32).T * 0.5).astype(BF16)
        pick4 = group_rows(4 * SAMP, 4).astype(BF16)
        w4t[...] = dot(pick4, w4_ref[...], 1, 0).astype(BF16)
        for r in range(given.shape[0]):
            lanes = slice(128 * r, 128 * (r + 1))
            given[r, 0:4, :] = delta_ref[:, lanes]
            given[r, 4:5, :] = count_ref[:, lanes].astype(F32)
            given[r, 5:8, :] = cot_ref[:, lanes]

    row16 = lax.broadcasted_iota(jnp.int32, (4 * SAMP, W), 0) & 3
    for part in range(tile // PART):
        rays = pl.ds(pl.multiple_of(step * tile + part * PART, PART), PART)
        wide = spread(x_ref[:, rays], jnp.zeros((), BF16))
        half = dot(w1t[...], wide, 1, 0)
        for k in range(3):
            hidden = (half + half * jnp.tanh(half)).astype(BF16)
            for s in range(SAMP):
                cols = slice(s * PART, (s + 1) * PART)
                put = slice(s * tile + part * PART, s * tile + (part + 1) * PART)
                if k == 0:
                    low_ref[0, :, put] = hidden[:, cols]
                else:
                    hid_ref[0, k - 1, :, put] = hidden[:, cols]
            if k < 2:
                half = dot(wmt[k], hidden, 1, 0)
        head = jnp.zeros((4 * SAMP, PART), F32)
        for s in range(SAMP):
            head += dot(
                jnp.where(row16 == s, w4t[...], jnp.zeros((), BF16)),
                hidden[:, s * PART : (s + 1) * PART], 1, 0,
            )
        for r in range(PART // 128):
            heads[step * (tile // 128) + part * (PART // 128) + r] = head[:, 128 * r : 128 * (r + 1)]

    @pl.when(step == pl.num_programs(0) - 1)
    def _():
        render(heads, given, ab_ref, pay_ref)


def render(heads, given, ab_ref, pay_ref):
    planes = heads.shape[0]
    zero = jnp.zeros((planes, 128), F32)
    counts = by_row(given, 4)
    cot = [by_row(given, 5 + c) for c in range(3)]
    reached, leaving = zero, jnp.ones((planes, 128), F32)
    share, left, facing, own = [], [], [], []
    for s in range(SAMP):
        raw = by_row(heads, s)
        density = jnp.maximum(raw, 0.0) + jnp.log1p(jnp.exp(-jnp.abs(raw)))
        span = jnp.where(counts > s, by_row(given, s), 0.0)
        reached = reached + density * span
        entering, leaving = leaving, jnp.exp(-reached)
        share.append(entering - leaving)
        left.append(leaving)
        own.append(span * jax.nn.sigmoid(raw))
        total = zero
        for c in range(3):
            albedo = jax.nn.sigmoid(by_row(heads, 4 * (c + 1) + s))
            lit = cot[c] * albedo
            total = total + lit
            ab_ref[4 * (c + 1) + s] = share[s] * lit * (1.0 - albedo)
        facing.append(total)
    later = zero
    for s in reversed(range(SAMP)):
        ab_ref[s] = (facing[s] * left[s] - later) * own[s]
        ab_ref[16 + s] = own[s]
        later = later + facing[s] * share[s]
    both = jnp.concatenate([-reached, later], axis=0)
    pay_ref[...] = jnp.broadcast_to(both[None], pay_ref.shape)


def slope_kernel(x_ref, low_hid, mid_hid, w1t, wmt, low_ref, mid_ref, top_ref):
    i = pl.program_id(0)
    x = x_ref[:, pl.ds(pl.multiple_of(i * TILE, TILE), TILE)]
    row = lax.broadcasted_iota(jnp.int32, x.shape, 0) & 3
    for s in range(SAMP):
        cols = slice(s * TILE, (s + 1) * TILE)
        wide = jnp.where(row == s, x, jnp.zeros((), BF16))
        for ref, weight, taken in (
            (low_ref, w1t[...], wide),
            (mid_ref, wmt[0], low_hid[0, :, cols]),
            (top_ref, wmt[1], mid_hid[0, 0, :, cols]),
        ):
            half = dot(weight, taken, 1, 0)
            curve = jnp.tanh(half)
            ref[0, :, cols] = (half + curve * (1.0 - half * curve)).astype(BF16)


def bend(back, slope):
    return (back + back * slope.astype(F32)).astype(BF16)


def split(place_ref, keep_ref, send_ref, pieces):
    for side in range(2):
        cols = slice(128 * side, 128 * (side + 1))

        def fill(ref):
            at = 0
            for piece in pieces:
                ref[at : at + piece.shape[0], :] = piece[:, cols]
                at += piece.shape[0]

        @pl.when(place_ref[1] == side)
        def _():
            fill(keep_ref)

        @pl.when(place_ref[1] != side)
        def _():
            fill(send_ref)


def top_kernel(
    place_ref, hid_hbm, slope_hbm, ab_ref, got_ref, rank_ref, w4_ref,
    back_ref, keep_ref, send_ref, hid, slope, front, heads, mid, last, w4h, sems,
):
    steps = hid.shape[0]

    def copies(i):
        return (
            pltpu.make_async_copy(slope_hbm.at[i], slope.at[i], sems.at[0, i]),
            pltpu.make_async_copy(hid_hbm.at[i], hid.at[i], sems.at[1, i]),
        )

    for i in range(steps):
        for copy in copies(i):
            copy.start()

    planes = rank_ref.shape[1]

    def one(v, _):
        mine = rank_ref[v]
        total = jnp.zeros((planes, 128), F32)
        for u in range(NV):
            total += jnp.where(rank_ref[u] < mine, got_ref[u, :planes], 0.0)
        front[v] = jnp.exp(total)
        return 0

    lax.fori_loop(0, NV, one, 0)
    me = place_ref[0]
    mine = rank_ref[me]
    behind = jnp.zeros((planes, 128), F32)
    for u in range(NV):
        behind += jnp.where(rank_ref[u] > mine, front[u] * got_ref[u, planes:], 0.0)
    prefix = front[me]
    rows = heads.reshape(planes * 4 * SAMP, 128)
    for r in range(4 * SAMP):
        value = ab_ref[r] * prefix
        if r < SAMP:
            value = value - ab_ref[16 + r] * behind
        rows[pl.ds(r, planes, stride=4 * SAMP), :] = value
    mid[...] = jnp.zeros_like(mid)
    last[...] = jnp.zeros_like(last)
    pick4 = (group_rows(4 * SAMP, 4).astype(F32) * 0.5).astype(BF16)
    w4h[...] = dot(w4_ref[...], pick4, 0, 1).astype(BF16)
    per = TILE // 128

    def step(i, _):
        for copy in copies(i):
            copy.wait()
        ghead = jnp.concatenate([heads[i * per + k] for k in range(per)], axis=1)
        ghead = spread(ghead.astype(BF16), jnp.zeros((), BF16))
        back = bend(dot(w4h[...], ghead, 1, 0), slope[i])
        back_ref[i] = back
        last[...] += dot(ghead, hid[i, 1], 1, 1)
        mid[...] += dot(hid[i, 0], back, 1, 1)
        return 0

    lax.fori_loop(0, steps, step, 0)
    pick8 = group_rows(4 * SAMP, 8).astype(F32)
    tail = dot(pick8, last[...], 0, 0, lax.Precision.HIGHEST)
    split(place_ref, keep_ref, send_ref, (mid[...], tail))


def middle_kernel(
    place_ref, hid_ref, slope_ref, back_ref, wm_ref, down_ref, keep_ref, send_ref, mid, halved
):
    mid[...] = jnp.zeros_like(mid)
    halved[...] = (wm_ref[1].astype(F32) * 0.5).astype(BF16)

    def step(i, _):
        down = bend(dot(halved[...], back_ref[i], 1, 0), slope_ref[i])
        down_ref[i] = down
        mid[...] += dot(hid_ref[i], down, 1, 1)
        return 0

    lax.fori_loop(0, hid_ref.shape[0], step, 0)
    split(place_ref, keep_ref, send_ref, (mid[...],))


def low_kernel(slope_ref, x_ref, back_ref, wm_ref, out_ref, first, halved):
    first[...] = jnp.zeros_like(first)
    halved[...] = (wm_ref[0].astype(F32) * 0.5).astype(BF16)

    def step(i, _):
        rays = pl.ds(pl.multiple_of(i * TILE, TILE), TILE)
        down = bend(dot(halved[...], back_ref[i], 1, 0), slope_ref[i])
        first[...] += dot(spread(x_ref[:, rays], jnp.zeros((), BF16)), down, 1, 1)
        return 0

    lax.fori_loop(0, slope_ref.shape[0], step, 0)
    pick = group_rows(FEAT * SAMP, FEAT).astype(F32)
    out_ref[...] = dot(pick, first[...], 0, 0, lax.Precision.HIGHEST)


def unpack_kernel(
    place_ref, a_ref, a_other, b_ref, b_other, c_ref, c_other, first_ref, mid_ref, last_ref
):
    first_ref[...] = c_ref[...] + c_other[...]
    for side in range(2):
        cols = slice(128 * side, 128 * (side + 1))

        def emit(up, down):
            mid_ref[1, :, cols] = up[0:256, :]
            last_ref[:, cols] = up[256:260, :]
            mid_ref[0, :, cols] = down[...]

        @pl.when(place_ref[1] == side)
        def _():
            emit(a_ref, b_ref)

        @pl.when(place_ref[1] != side)
        def _():
            emit(a_other, b_other)


def far(value):
    return pltpu.with_memory_space_constraint(value, HBM)


def near(value):
    return pltpu.with_memory_space_constraint(value, VMEM)


def forward(x, deltas, counts, cot, w1, wm, w4):
    rays = x.shape[1]
    whole2 = lambda i: (0, 0)
    inside = pl.BlockSpec(memory_space=VMEM)
    return pl.pallas_call(
        forward_kernel,
        grid=(rays // TILE,),
        in_specs=[
            inside,
            pl.BlockSpec((SAMP, rays), whole2),
            pl.BlockSpec((1, rays), whole2),
            pl.BlockSpec((3, rays), whole2),
            pl.BlockSpec((FEAT, W), whole2),
            pl.BlockSpec((2, W, W), lambda i: (0, 0, 0)),
            pl.BlockSpec((4, W), whole2),
        ],
        out_specs=[
            pl.BlockSpec((1, 2, W, SAMP * TILE), lambda i: (i, 0, 0, 0)),
            pl.BlockSpec((1, W, SAMP * TILE), lambda i: (i, 0, 0)),
        ] + [inside] * 4,
        out_shape=[
            pltpu.HBM((rays // TILE, 2, W, SAMP * TILE), BF16),
            pltpu.HBM((rays // TILE, W, SAMP * TILE), BF16),
            pltpu.VMEM((20, rays // 128, 128), F32),
            pltpu.VMEM((NV, 2 * rays // 128, 128), F32),
            pltpu.VMEM((W, FEAT * SAMP), BF16),
            pltpu.VMEM((2, W, W), BF16),
        ],
        scratch_shapes=[
            pltpu.VMEM((4 * SAMP, W), BF16),
            pltpu.VMEM((rays // 128, 4 * SAMP, 128), F32),
            pltpu.VMEM((rays // 128, 8, 128), F32),
        ],
        compiler_params=pltpu.CompilerParams(vmem_limit_bytes=40 * MIB),
        cost_estimate=pl.CostEstimate(
            flops=2 * SAMP * rays * 140288, transcendentals=3 * W * SAMP * rays,
            bytes_accessed=MIB,
        ),
        name="forward",
    )(near(x), far(deltas), far(counts), far(cot), far(w1), far(wm), far(w4))


def slopes(x, low_hid, hid, w1t, wmt):
    steps, _, _, n = hid.shape
    block = pl.BlockSpec((1, W, n), lambda i: (i, 0, 0))
    inside = pl.BlockSpec(memory_space=VMEM)
    return pl.pallas_call(
        slope_kernel,
        grid=(steps,),
        in_specs=[
            inside,
            block,
            pl.BlockSpec((1, 1, W, n), lambda i: (i, 0, 0, 0)),
            inside, inside,
        ],
        out_specs=[block] * 3,
        out_shape=[pltpu.HBM((steps, W, n), BF16)] * 3,
        compiler_params=pltpu.CompilerParams(vmem_limit_bytes=LIMIT),
        cost_estimate=pl.CostEstimate(
            flops=2 * steps * n * 140000, transcendentals=3 * W * steps * n,
            bytes_accessed=20 * MIB,
        ),
        name="slopes",
    )(near(x), far(low_hid), far(hid), near(w1t), near(wmt))


def top(place, hid, slope, ab, got, ranks, w4):
    inside = pl.BlockSpec(memory_space=VMEM)
    steps, _, _, n = hid.shape
    return pl.pallas_call(
        top_kernel,
        in_specs=[pl.BlockSpec(memory_space=SMEM)] + [pl.BlockSpec(memory_space=HBM)] * 2 + [inside] * 4,
        out_specs=[inside] * 3,
        out_shape=[
            pltpu.VMEM((steps, W, n), BF16),
            pltpu.VMEM((264, 128), F32),
            pltpu.VMEM((264, 128), F32),
        ],
        scratch_shapes=[
            pltpu.VMEM(hid.shape, BF16),
            pltpu.VMEM(slope.shape, BF16),
            pltpu.VMEM((NV,) + ab.shape[1:], F32),
            pltpu.VMEM((ab.shape[1], 4 * SAMP, 128), F32),
            pltpu.VMEM((W, W), F32),
            pltpu.VMEM((4 * SAMP, W), F32),
            pltpu.VMEM((W, 4 * SAMP), BF16),
            pltpu.SemaphoreType.DMA((2, steps)),
        ],
        compiler_params=pltpu.CompilerParams(vmem_limit_bytes=24 * MIB),
        cost_estimate=pl.CostEstimate(
            flops=2 * steps * n * 80000, transcendentals=0, bytes_accessed=12 * MIB
        ),
        name="top",
    )(place, far(hid), far(slope), near(ab), near(got), near(ranks), near(w4))


def middle(place, hid, slope, back, wm):
    inside = pl.BlockSpec(memory_space=VMEM)
    steps, _, n = hid.shape
    return pl.pallas_call(
        middle_kernel,
        in_specs=[pl.BlockSpec(memory_space=SMEM)] + [inside] * 4,
        out_specs=[inside] * 3,
        out_shape=[
            pltpu.VMEM((steps, W, n), BF16),
            pltpu.VMEM((256, 128), F32),
            pltpu.VMEM((256, 128), F32),
        ],
        scratch_shapes=[pltpu.VMEM((W, W), F32), pltpu.VMEM((W, W), BF16)],
        compiler_params=pltpu.CompilerParams(vmem_limit_bytes=12 * MIB),
        cost_estimate=pl.CostEstimate(
            flops=2 * steps * n * 131072, transcendentals=0, bytes_accessed=8 * MIB
        ),
        name="middle",
    )(place, near(hid), near(slope), near(back), near(wm))


def low(slope, x, back, wm):
    inside = pl.BlockSpec(memory_space=VMEM)
    steps, _, n = slope.shape
    return pl.pallas_call(
        low_kernel,
        in_specs=[inside] * 4,
        out_specs=inside,
        out_shape=pltpu.VMEM((FEAT, W), F32),
        scratch_shapes=[pltpu.VMEM((FEAT * SAMP, W), F32), pltpu.VMEM((W, W), BF16)],
        compiler_params=pltpu.CompilerParams(vmem_limit_bytes=12 * MIB),
        cost_estimate=pl.CostEstimate(
            flops=2 * steps * n * 90000, transcendentals=0, bytes_accessed=8 * MIB
        ),
        name="low",
    )(near(slope), near(x), near(back), near(wm))


def unpack(place, *parts):
    inside = pl.BlockSpec(memory_space=VMEM)
    return pl.pallas_call(
        unpack_kernel,
        grid=(1,),
        in_specs=[pl.BlockSpec(memory_space=SMEM)] + [inside] * 6,
        out_specs=[
            pl.BlockSpec((FEAT, W), lambda i: (0, 0)),
            pl.BlockSpec((2, W, W), lambda i: (0, 0, 0)),
            pl.BlockSpec((4, W), lambda i: (0, 0)),
        ],
        out_shape=[
            pltpu.HBM((FEAT, W), F32),
            pltpu.HBM((2, W, W), F32),
            pltpu.HBM((4, W), F32),
        ],
        compiler_params=pltpu.CompilerParams(vmem_limit_bytes=12 * MIB),
        name="unpack",
    )(place, *map(near, parts))


PAIR = [(0, 1), (1, 0)]
NEAR = [(0, 1), (1, 0), (2, 3), (3, 2)]
FAR = [(0, 3), (3, 0), (1, 2), (2, 1)]


def over_cores(keep, send):
    got = lax.ppermute(send, "core", PAIR)
    return keep + got


def over_x(value, ring):
    got = lax.ppermute(value, "x", ring)
    return value + got


def per_device(
    features, deltas, counts, order_rank, cotangent, first_weight, middle_weight, last_weight
):
    x = features[0].reshape(FEAT * SAMP, -1)
    place = jnp.stack([lax.axis_index(("z", "y")), lax.axis_index("core")]).astype(jnp.int32)
    ranks = order_rank.T.reshape(NV, -1, 128)
    w1, wm, w4 = first_weight[0], middle_weight[0], last_weight[0].T
    hid, low_hid, ab, pay, w1t, wmt = forward(x, deltas[0], counts, cotangent, w1, wm, w4)
    got = lax.all_to_all(pay, ("z", "y"), 0, 0, tiled=True)
    low_slope, mid_slope, top_slope = slopes(x, low_hid, hid, w1t, wmt)
    back, *sums = top(place, hid, top_slope, ab, got, ranks, w4)
    upper = over_x(over_cores(*sums), NEAR)
    back, *sums = middle(place, low_hid, mid_slope, back, wm)
    upper = over_x(upper, FAR)
    lower = over_x(over_cores(*sums), NEAR)
    small = low(low_slope, x, back, wm)
    small = small + sum(
        lax.ppermute(small, "x", [(i, (i + s) % 4) for i in range(4)]) for s in (1, 2, 3)
    )
    lower = over_x(lower, FAR)
    parts = []
    for part in (upper, lower, small):
        parts += [part, lax.ppermute(part, "core", PAIR)]
    first, mid, last = unpack(place, *parts)
    return (first[None], mid[None], last.T[None])


def solution(mesh):
    fine = Mesh(mesh.devices.reshape(8, 4, 4, 2), ("z", "y", "x", "core"))
    vol, rep = ("z", "y"), ("x", "core")
    placed = (
        P(vol, None, None, rep),
        P(vol, None, rep),
        P(vol, rep),
        P(rep, None),
        P(None, rep),
        P(vol, None, None),
        P(vol, None, None, None),
        P(vol, None, None),
    )
    return jax.shard_map(
        per_device,
        mesh=fine,
        in_specs=placed,
        out_specs=(P(vol, None, None), P(vol, None, None, None), P(vol, None, None)),
        check_vma=False,
    )
```

```python
import jax
import jax.numpy as jnp
from jax import lax
from jax.experimental import pallas as pl
from jax.experimental.pallas import tpu as pltpu
from jax.sharding import Mesh, PartitionSpec as P


F32 = jnp.float32
BF16 = jnp.bfloat16
TILE = 512
PART = 256
SAMP = 4
FEAT = 32
W = 256
NV = 32
MIB = 1024 * 1024
HBM = pltpu.MemorySpace.HBM
VMEM = pltpu.MemorySpace.VMEM
SMEM = pltpu.MemorySpace.SMEM
LIMIT = 24 * MIB


def dot(lhs, rhs, lhs_dim, rhs_dim, precision=None):
    return lax.dot_general(
        lhs, rhs, (((lhs_dim,), (rhs_dim,)), ((), ())),
        preferred_element_type=F32, precision=precision,
    )


def group_rows(rows, width):
    i = lax.broadcasted_iota(jnp.int32, (rows, width), 0)
    j = lax.broadcasted_iota(jnp.int32, (rows, width), 1)
    return lax.shift_right_logical(i, 2) == j


def spread(block, fill):
    row = lax.broadcasted_iota(jnp.int32, block.shape, 0)
    parts = [jnp.where((row & 3) == s, block, fill) for s in range(SAMP)]
    return jnp.concatenate(parts, axis=1)


def by_row(ref, row):
    planes, rows, _ = ref.shape
    return ref.reshape(planes * rows, 128)[pl.ds(row, planes, stride=rows), :]


def forward_kernel(
    x_ref, delta_ref, count_ref, cot_ref, w1_ref, wm_ref, w4_ref,
    hid_ref, low_ref, ab_ref, pay_ref, w1t, wmt, w4t, heads, given,
):
    step = pl.program_id(0)
    tile = TILE

    @pl.when(step == 0)
    def _():
        pick = group_rows(FEAT * SAMP, FEAT).astype(BF16)
        w1t[...] = (dot(w1_ref[...], pick, 0, 1) * 0.5).astype(BF16)
        for k in range(2):
            wmt[k] = (wm_ref[k].astype(F32).T * 0.5).astype(BF16)
        pick4 = group_rows(4 * SAMP, 4).astype(BF16)
        w4t[...] = dot(pick4, w4_ref[...], 1, 0).astype(BF16)
        for r in range(given.shape[0]):
            lanes = slice(128 * r, 128 * (r + 1))
            given[r, 0:4, :] = delta_ref[:, lanes]
            given[r, 4:5, :] = count_ref[:, lanes].astype(F32)
            given[r, 5:8, :] = cot_ref[:, lanes]

    row16 = lax.broadcasted_iota(jnp.int32, (4 * SAMP, W), 0) & 3
    parts = range(tile // PART)
    halves = []
    for part in parts:
        rays = pl.ds(pl.multiple_of(step * tile + part * PART, PART), PART)
        halves.append(dot(w1t[...], spread(x_ref[:, rays], jnp.zeros((), BF16)), 1, 0))
    for k in range(3):
        hiddens = []
        for part in parts:
            half = halves[part]
            hidden = (half + half * jnp.tanh(half)).astype(BF16)
            hiddens.append(hidden)
            for s in range(SAMP):
                cols = slice(s * PART, (s + 1) * PART)
                put = slice(s * tile + part * PART, s * tile + (part + 1) * PART)
                if k == 0:
                    low_ref[0, :, put] = hidden[:, cols]
                else:
                    hid_ref[0, k - 1, :, put] = hidden[:, cols]
            if k < 2:
                halves[part] = dot(wmt[k], hidden, 1, 0)
    for part in parts:
        head = jnp.zeros((4 * SAMP, PART), F32)
        for s in range(SAMP):
            head += dot(
                jnp.where(row16 == s, w4t[...], jnp.zeros((), BF16)),
                hiddens[part][:, s * PART : (s + 1) * PART], 1, 0,
            )
        for r in range(PART // 128):
            heads[step * (tile // 128) + part * (PART // 128) + r] = head[:, 128 * r : 128 * (r + 1)]

    @pl.when(step == pl.num_programs(0) - 1)
    def _():
        render(heads, given, ab_ref, pay_ref)


def render(heads, given, ab_ref, pay_ref):
    planes = heads.shape[0]
    zero = jnp.zeros((planes, 128), F32)
    counts = by_row(given, 4)
    cot = [by_row(given, 5 + c) for c in range(3)]
    reached, leaving = zero, jnp.ones((planes, 128), F32)
    share, left, facing, own = [], [], [], []
    for s in range(SAMP):
        raw = by_row(heads, s)
        density = jnp.maximum(raw, 0.0) + jnp.log1p(jnp.exp(-jnp.abs(raw)))
        span = jnp.where(counts > s, by_row(given, s), 0.0)
        reached = reached + density * span
        entering, leaving = leaving, jnp.exp(-reached)
        share.append(entering - leaving)
        left.append(leaving)
        own.append(span * jax.nn.sigmoid(raw))
        total = zero
        for c in range(3):
            albedo = jax.nn.sigmoid(by_row(heads, 4 * (c + 1) + s))
            lit = cot[c] * albedo
            total = total + lit
            ab_ref[4 * (c + 1) + s] = share[s] * lit * (1.0 - albedo)
        facing.append(total)
    later = zero
    for s in reversed(range(SAMP)):
        ab_ref[s] = (facing[s] * left[s] - later) * own[s]
        ab_ref[16 + s] = own[s]
        later = later + facing[s] * share[s]
    both = jnp.concatenate([-reached, later], axis=0)
    pay_ref[...] = jnp.broadcast_to(both[None], pay_ref.shape)


def slope_kernel(x_ref, low_hid, mid_hid, w1t, wmt, low_ref, mid_ref, top_ref):
    i = pl.program_id(0)
    x = x_ref[:, pl.ds(pl.multiple_of(i * TILE, TILE), TILE)]
    row = lax.broadcasted_iota(jnp.int32, x.shape, 0) & 3
    for s in range(SAMP):
        cols = slice(s * TILE, (s + 1) * TILE)
        wide = jnp.where(row == s, x, jnp.zeros((), BF16))
        for ref, weight, taken in (
            (low_ref, w1t[...], wide),
            (mid_ref, wmt[0], low_hid[0, :, cols]),
            (top_ref, wmt[1], mid_hid[0, 0, :, cols]),
        ):
            half = dot(weight, taken, 1, 0)
            curve = jnp.tanh(half)
            ref[0, :, cols] = (half + curve * (1.0 - half * curve)).astype(BF16)


def bend(back, slope):
    return (back + back * slope.astype(F32)).astype(BF16)


def split(place_ref, keep_ref, send_ref, pieces):
    for side in range(2):
        cols = slice(128 * side, 128 * (side + 1))

        def fill(ref):
            at = 0
            for piece in pieces:
                ref[at : at + piece.shape[0], :] = piece[:, cols]
                at += piece.shape[0]

        @pl.when(place_ref[1] == side)
        def _():
            fill(keep_ref)

        @pl.when(place_ref[1] != side)
        def _():
            fill(send_ref)


def top_kernel(
    place_ref, hid_hbm, slope_hbm, ab_ref, got_ref, rank_ref, w4_ref,
    back_ref, keep_ref, send_ref, hid, slope, front, heads, mid, last, w4h, sems,
):
    steps = hid.shape[0]

    def copies(i):
        return (
            pltpu.make_async_copy(slope_hbm.at[i], slope.at[i], sems.at[0, i]),
            pltpu.make_async_copy(hid_hbm.at[i], hid.at[i], sems.at[1, i]),
        )

    for i in range(steps):
        for copy in copies(i):
            copy.start()

    planes = rank_ref.shape[1]

    def one(v, _):
        mine = rank_ref[v]
        total = jnp.zeros((planes, 128), F32)
        for u in range(NV):
            total += jnp.where(rank_ref[u] < mine, got_ref[u, :planes], 0.0)
        front[v] = jnp.exp(total)
        return 0

    lax.fori_loop(0, NV, one, 0)
    me = place_ref[0]
    mine = rank_ref[me]
    behind = jnp.zeros((planes, 128), F32)
    for u in range(NV):
        behind += jnp.where(rank_ref[u] > mine, front[u] * got_ref[u, planes:], 0.0)
    prefix = front[me]
    rows = heads.reshape(planes * 4 * SAMP, 128)
    for r in range(4 * SAMP):
        value = ab_ref[r] * prefix
        if r < SAMP:
            value = value - ab_ref[16 + r] * behind
        rows[pl.ds(r, planes, stride=4 * SAMP), :] = value
    mid[...] = jnp.zeros_like(mid)
    last[...] = jnp.zeros_like(last)
    pick4 = (group_rows(4 * SAMP, 4).astype(F32) * 0.5).astype(BF16)
    w4h[...] = dot(w4_ref[...], pick4, 0, 1).astype(BF16)
    per = TILE // 128

    def step(i, _):
        for copy in copies(i):
            copy.wait()
        ghead = jnp.concatenate([heads[i * per + k] for k in range(per)], axis=1)
        ghead = spread(ghead.astype(BF16), jnp.zeros((), BF16))
        back = bend(dot(w4h[...], ghead, 1, 0), slope[i])
        back_ref[i] = back
        last[...] += dot(ghead, hid[i, 1], 1, 1)
        mid[...] += dot(hid[i, 0], back, 1, 1)
        return 0

    lax.fori_loop(0, steps, step, 0, unroll=2)
    pick8 = group_rows(4 * SAMP, 8).astype(F32)
    tail = dot(pick8, last[...], 0, 0, lax.Precision.HIGHEST)
    split(place_ref, keep_ref, send_ref, (mid[...], tail))


def middle_kernel(
    place_ref, hid_ref, slope_ref, back_ref, wm_ref, down_ref, keep_ref, send_ref, mid, halved
):
    mid[...] = jnp.zeros_like(mid)
    halved[...] = (wm_ref[1].astype(F32) * 0.5).astype(BF16)

    def step(i, _):
        down = bend(dot(halved[...], back_ref[i], 1, 0), slope_ref[i])
        down_ref[i] = down
        mid[...] += dot(hid_ref[i], down, 1, 1)
        return 0

    lax.fori_loop(0, hid_ref.shape[0], step, 0, unroll=2)
    split(place_ref, keep_ref, send_ref, (mid[...],))


def low_kernel(slope_ref, x_ref, back_ref, wm_ref, out_ref, first, halved):
    first[...] = jnp.zeros_like(first)
    halved[...] = (wm_ref[0].astype(F32) * 0.5).astype(BF16)

    def step(i, _):
        rays = pl.ds(pl.multiple_of(i * TILE, TILE), TILE)
        down = bend(dot(halved[...], back_ref[i], 1, 0), slope_ref[i])
        first[...] += dot(spread(x_ref[:, rays], jnp.zeros((), BF16)), down, 1, 1)
        return 0

    lax.fori_loop(0, slope_ref.shape[0], step, 0, unroll=2)
    pick = group_rows(FEAT * SAMP, FEAT).astype(F32)
    out_ref[...] = dot(pick, first[...], 0, 0, lax.Precision.HIGHEST)


def unpack_kernel(
    place_ref, a_ref, a_other, b_ref, b_other, c_ref, c_other, first_ref, mid_ref, last_ref
):
    first_ref[...] = c_ref[...] + c_other[...]
    for side in range(2):
        cols = slice(128 * side, 128 * (side + 1))

        def emit(up, down):
            mid_ref[1, :, cols] = up[0:256, :]
            last_ref[:, cols] = up[256:260, :]
            mid_ref[0, :, cols] = down[...]

        @pl.when(place_ref[1] == side)
        def _():
            emit(a_ref, b_ref)

        @pl.when(place_ref[1] != side)
        def _():
            emit(a_other, b_other)


def far(value):
    return pltpu.with_memory_space_constraint(value, HBM)


def near(value):
    return pltpu.with_memory_space_constraint(value, VMEM)


def forward(x, deltas, counts, cot, w1, wm, w4):
    rays = x.shape[1]
    whole2 = lambda i: (0, 0)
    inside = pl.BlockSpec(memory_space=VMEM)
    return pl.pallas_call(
        forward_kernel,
        grid=(rays // TILE,),
        in_specs=[
            inside,
            pl.BlockSpec((SAMP, rays), whole2),
            pl.BlockSpec((1, rays), whole2),
            pl.BlockSpec((3, rays), whole2),
            pl.BlockSpec((FEAT, W), whole2),
            pl.BlockSpec((2, W, W), lambda i: (0, 0, 0)),
            pl.BlockSpec((4, W), whole2),
        ],
        out_specs=[
            pl.BlockSpec((1, 2, W, SAMP * TILE), lambda i: (i, 0, 0, 0)),
            pl.BlockSpec((1, W, SAMP * TILE), lambda i: (i, 0, 0)),
        ] + [inside] * 4,
        out_shape=[
            pltpu.HBM((rays // TILE, 2, W, SAMP * TILE), BF16),
            pltpu.HBM((rays // TILE, W, SAMP * TILE), BF16),
            pltpu.VMEM((20, rays // 128, 128), F32),
            pltpu.VMEM((NV, 2 * rays // 128, 128), F32),
            pltpu.VMEM((W, FEAT * SAMP), BF16),
            pltpu.VMEM((2, W, W), BF16),
        ],
        scratch_shapes=[
            pltpu.VMEM((4 * SAMP, W), BF16),
            pltpu.VMEM((rays // 128, 4 * SAMP, 128), F32),
            pltpu.VMEM((rays // 128, 8, 128), F32),
        ],
        compiler_params=pltpu.CompilerParams(vmem_limit_bytes=40 * MIB),
        cost_estimate=pl.CostEstimate(
            flops=2 * SAMP * rays * 140288, transcendentals=3 * W * SAMP * rays,
            bytes_accessed=MIB,
        ),
        name="forward",
    )(near(x), far(deltas), far(counts), far(cot), far(w1), far(wm), far(w4))


def slopes(x, low_hid, hid, w1t, wmt):
    steps, _, _, n = hid.shape
    block = pl.BlockSpec((1, W, n), lambda i: (i, 0, 0))
    inside = pl.BlockSpec(memory_space=VMEM)
    return pl.pallas_call(
        slope_kernel,
        grid=(steps,),
        in_specs=[
            inside,
            block,
            pl.BlockSpec((1, 1, W, n), lambda i: (i, 0, 0, 0)),
            inside, inside,
        ],
        out_specs=[block] * 3,
        out_shape=[pltpu.HBM((steps, W, n), BF16)] * 3,
        compiler_params=pltpu.CompilerParams(vmem_limit_bytes=LIMIT),
        cost_estimate=pl.CostEstimate(
            flops=2 * steps * n * 140000, transcendentals=3 * W * steps * n,
            bytes_accessed=20 * MIB,
        ),
        name="slopes",
    )(near(x), far(low_hid), far(hid), near(w1t), near(wmt))


def top(place, hid, slope, ab, got, ranks, w4):
    inside = pl.BlockSpec(memory_space=VMEM)
    steps, _, _, n = hid.shape
    return pl.pallas_call(
        top_kernel,
        in_specs=[pl.BlockSpec(memory_space=SMEM)] + [pl.BlockSpec(memory_space=HBM)] * 2 + [inside] * 4,
        out_specs=[inside] * 3,
        out_shape=[
            pltpu.VMEM((steps, W, n), BF16),
            pltpu.VMEM((264, 128), F32),
            pltpu.VMEM((264, 128), F32),
        ],
        scratch_shapes=[
            pltpu.VMEM(hid.shape, BF16),
            pltpu.VMEM(slope.shape, BF16),
            pltpu.VMEM((NV,) + ab.shape[1:], F32),
            pltpu.VMEM((ab.shape[1], 4 * SAMP, 128), F32),
            pltpu.VMEM((W, W), F32),
            pltpu.VMEM((4 * SAMP, W), F32),
            pltpu.VMEM((W, 4 * SAMP), BF16),
            pltpu.SemaphoreType.DMA((2, steps)),
        ],
        compiler_params=pltpu.CompilerParams(vmem_limit_bytes=24 * MIB),
        cost_estimate=pl.CostEstimate(
            flops=2 * steps * n * 80000, transcendentals=0, bytes_accessed=12 * MIB
        ),
        name="top",
    )(place, far(hid), far(slope), near(ab), near(got), near(ranks), near(w4))


def middle(place, hid, slope, back, wm):
    inside = pl.BlockSpec(memory_space=VMEM)
    steps, _, n = hid.shape
    return pl.pallas_call(
        middle_kernel,
        in_specs=[pl.BlockSpec(memory_space=SMEM)] + [inside] * 4,
        out_specs=[inside] * 3,
        out_shape=[
            pltpu.VMEM((steps, W, n), BF16),
            pltpu.VMEM((256, 128), F32),
            pltpu.VMEM((256, 128), F32),
        ],
        scratch_shapes=[pltpu.VMEM((W, W), F32), pltpu.VMEM((W, W), BF16)],
        compiler_params=pltpu.CompilerParams(vmem_limit_bytes=12 * MIB),
        cost_estimate=pl.CostEstimate(
            flops=2 * steps * n * 131072, transcendentals=0, bytes_accessed=8 * MIB
        ),
        name="middle",
    )(place, near(hid), near(slope), near(back), near(wm))


def low(slope, x, back, wm):
    inside = pl.BlockSpec(memory_space=VMEM)
    steps, _, n = slope.shape
    return pl.pallas_call(
        low_kernel,
        in_specs=[inside] * 4,
        out_specs=inside,
        out_shape=pltpu.VMEM((FEAT, W), F32),
        scratch_shapes=[pltpu.VMEM((FEAT * SAMP, W), F32), pltpu.VMEM((W, W), BF16)],
        compiler_params=pltpu.CompilerParams(vmem_limit_bytes=12 * MIB),
        cost_estimate=pl.CostEstimate(
            flops=2 * steps * n * 90000, transcendentals=0, bytes_accessed=8 * MIB
        ),
        name="low",
    )(near(slope), near(x), near(back), near(wm))


def unpack(place, *parts):
    inside = pl.BlockSpec(memory_space=VMEM)
    return pl.pallas_call(
        unpack_kernel,
        grid=(1,),
        in_specs=[pl.BlockSpec(memory_space=SMEM)] + [inside] * 6,
        out_specs=[
            pl.BlockSpec((FEAT, W), lambda i: (0, 0)),
            pl.BlockSpec((2, W, W), lambda i: (0, 0, 0)),
            pl.BlockSpec((4, W), lambda i: (0, 0)),
        ],
        out_shape=[
            pltpu.HBM((FEAT, W), F32),
            pltpu.HBM((2, W, W), F32),
            pltpu.HBM((4, W), F32),
        ],
        compiler_params=pltpu.CompilerParams(vmem_limit_bytes=12 * MIB),
        name="unpack",
    )(place, *map(near, parts))


PAIR = [(0, 1), (1, 0)]
NEAR = [(0, 1), (1, 0), (2, 3), (3, 2)]
FAR = [(0, 3), (3, 0), (1, 2), (2, 1)]


def over_cores(keep, send):
    got = lax.ppermute(send, "core", PAIR)
    return keep + got


def over_x(value, ring):
    got = lax.ppermute(value, "x", ring)
    return value + got


def per_device(
    features, deltas, counts, order_rank, cotangent, first_weight, middle_weight, last_weight
):
    x = features[0].reshape(FEAT * SAMP, -1)
    place = jnp.stack([lax.axis_index(("z", "y")), lax.axis_index("core")]).astype(jnp.int32)
    ranks = order_rank.T.reshape(NV, -1, 128)
    w1, wm, w4 = first_weight[0], middle_weight[0], last_weight[0].T
    hid, low_hid, ab, pay, w1t, wmt = forward(x, deltas[0], counts, cotangent, w1, wm, w4)
    got = lax.all_to_all(pay, ("z", "y"), 0, 0, tiled=True)
    low_slope, mid_slope, top_slope = slopes(x, low_hid, hid, w1t, wmt)
    back, *sums = top(place, hid, top_slope, ab, got, ranks, w4)
    upper = over_x(over_cores(*sums), NEAR)
    back, *sums = middle(place, low_hid, mid_slope, back, wm)
    lower = over_x(over_cores(*sums), FAR)
    small = low(low_slope, x, back, wm)
    upper = over_x(upper, FAR)
    small = small + sum(
        lax.ppermute(small, "x", [(i, (i + s) % 4) for i in range(4)]) for s in (1, 2, 3)
    )
    lower = over_x(lower, NEAR)
    parts = []
    for part in (upper, lower, small):
        parts += [part, lax.ppermute(part, "core", PAIR)]
    first, mid, last = unpack(place, *parts)
    return (first[None], mid[None], last.T[None])


def solution(mesh):
    fine = Mesh(mesh.devices.reshape(8, 4, 4, 2), ("z", "y", "x", "core"))
    vol, rep = ("z", "y"), ("x", "core")
    placed = (
        P(vol, None, None, rep),
        P(vol, None, rep),
        P(vol, rep),
        P(rep, None),
        P(None, rep),
        P(vol, None, None),
        P(vol, None, None, None),
        P(vol, None, None),
    )
    return jax.shard_map(
        per_device,
        mesh=fine,
        in_specs=placed,
        out_specs=(P(vol, None, None), P(vol, None, None, None), P(vol, None, None)),
        check_vma=False,
    )
```

```python
import jax
import jax.numpy as jnp
from jax import lax
from jax.experimental import pallas as pl
from jax.experimental.pallas import tpu as pltpu
from jax.sharding import Mesh, PartitionSpec as P


F32 = jnp.float32
BF16 = jnp.bfloat16
TILE = 512
PART = 256
SAMP = 4
FEAT = 32
W = 256
NV = 32
MIB = 1024 * 1024
HBM = pltpu.MemorySpace.HBM
VMEM = pltpu.MemorySpace.VMEM
SMEM = pltpu.MemorySpace.SMEM
LIMIT = 24 * MIB


def dot(lhs, rhs, lhs_dim, rhs_dim, precision=None):
    return lax.dot_general(
        lhs, rhs, (((lhs_dim,), (rhs_dim,)), ((), ())),
        preferred_element_type=F32, precision=precision,
    )


def group_rows(rows, width):
    i = lax.broadcasted_iota(jnp.int32, (rows, width), 0)
    j = lax.broadcasted_iota(jnp.int32, (rows, width), 1)
    return lax.shift_right_logical(i, 2) == j


def spread(block, fill):
    row = lax.broadcasted_iota(jnp.int32, block.shape, 0)
    parts = [jnp.where((row & 3) == s, block, fill) for s in range(SAMP)]
    return jnp.concatenate(parts, axis=1)


def by_row(ref, row):
    planes, rows, _ = ref.shape
    return ref.reshape(planes * rows, 128)[pl.ds(row, planes, stride=rows), :]


def forward_kernel(
    x_ref, delta_ref, count_ref, cot_ref, w1_ref, wm_ref, w4_ref,
    hid_ref, low_ref, ab_ref, pay_ref, w1t, wmt, w4t, heads, given,
):
    step = pl.program_id(0)
    tile = TILE

    @pl.when(step == 0)
    def _():
        pick = group_rows(FEAT * SAMP, FEAT).astype(BF16)
        w1t[...] = (dot(w1_ref[...], pick, 0, 1) * 0.5).astype(BF16)
        for k in range(2):
            wmt[k] = (wm_ref[k].astype(F32).T * 0.5).astype(BF16)
        pick4 = group_rows(4 * SAMP, 4).astype(BF16)
        w4t[...] = dot(pick4, w4_ref[...], 1, 0).astype(BF16)
        for r in range(given.shape[0]):
            lanes = slice(128 * r, 128 * (r + 1))
            given[r, 0:4, :] = delta_ref[:, lanes]
            given[r, 4:5, :] = count_ref[:, lanes].astype(F32)
            given[r, 5:8, :] = cot_ref[:, lanes]

    row16 = lax.broadcasted_iota(jnp.int32, (4 * SAMP, W), 0) & 3
    parts = range(tile // PART)
    halves = []
    for part in parts:
        rays = pl.ds(pl.multiple_of(step * tile + part * PART, PART), PART)
        halves.append(dot(w1t[...], spread(x_ref[:, rays], jnp.zeros((), BF16)), 1, 0))
    for k in range(3):
        hiddens = []
        for part in parts:
            half = halves[part]
            hidden = (half + half * jnp.tanh(half)).astype(BF16)
            hiddens.append(hidden)
            for s in range(SAMP):
                cols = slice(s * PART, (s + 1) * PART)
                put = slice(s * tile + part * PART, s * tile + (part + 1) * PART)
                if k == 0:
                    low_ref[0, :, put] = hidden[:, cols]
                else:
                    hid_ref[0, k - 1, :, put] = hidden[:, cols]
            if k < 2:
                halves[part] = dot(wmt[k], hidden, 1, 0)
    for part in parts:
        head = jnp.zeros((4 * SAMP, PART), F32)
        for s in range(SAMP):
            head += dot(
                jnp.where(row16 == s, w4t[...], jnp.zeros((), BF16)),
                hiddens[part][:, s * PART : (s + 1) * PART], 1, 0,
            )
        for r in range(PART // 128):
            heads[step * (tile // 128) + part * (PART // 128) + r] = head[:, 128 * r : 128 * (r + 1)]

    @pl.when(step == pl.num_programs(0) - 1)
    def _():
        render(heads, given, ab_ref, pay_ref)


def render(heads, given, ab_ref, pay_ref):
    planes = heads.shape[0]
    zero = jnp.zeros((planes, 128), F32)
    counts = by_row(given, 4)
    cot = [by_row(given, 5 + c) for c in range(3)]
    reached, leaving = zero, jnp.ones((planes, 128), F32)
    share, left, facing, own = [], [], [], []
    for s in range(SAMP):
        raw = by_row(heads, s)
        density = jnp.maximum(raw, 0.0) + jnp.log1p(jnp.exp(-jnp.abs(raw)))
        span = jnp.where(counts > s, by_row(given, s), 0.0)
        reached = reached + density * span
        entering, leaving = leaving, jnp.exp(-reached)
        share.append(entering - leaving)
        left.append(leaving)
        own.append(span * jax.nn.sigmoid(raw))
        total = zero
        for c in range(3):
            albedo = jax.nn.sigmoid(by_row(heads, 4 * (c + 1) + s))
            lit = cot[c] * albedo
            total = total + lit
            ab_ref[4 * (c + 1) + s] = share[s] * lit * (1.0 - albedo)
        facing.append(total)
    later = zero
    for s in reversed(range(SAMP)):
        ab_ref[s] = (facing[s] * left[s] - later) * own[s]
        ab_ref[16 + s] = own[s]
        later = later + facing[s] * share[s]
    both = jnp.concatenate([-reached, later], axis=0)
    pay_ref[...] = jnp.broadcast_to(both[None], pay_ref.shape)


def slope_kernel(x_ref, low_hid, mid_hid, w1t, wmt, low_ref, mid_ref, top_ref):
    i = pl.program_id(0)
    x = x_ref[:, pl.ds(pl.multiple_of(i * TILE, TILE), TILE)]
    row = lax.broadcasted_iota(jnp.int32, x.shape, 0) & 3
    for s in range(SAMP):
        cols = slice(s * TILE, (s + 1) * TILE)
        wide = jnp.where(row == s, x, jnp.zeros((), BF16))
        for ref, weight, taken in (
            (low_ref, w1t[...], wide),
            (mid_ref, wmt[0], low_hid[0, :, cols]),
            (top_ref, wmt[1], mid_hid[0, 0, :, cols]),
        ):
            half = dot(weight, taken, 1, 0)
            curve = jnp.tanh(half)
            ref[0, :, cols] = (half + curve * (1.0 - half * curve)).astype(BF16)


def bend(back, slope):
    return (back + back * slope.astype(F32)).astype(BF16)


def split(place_ref, keep_ref, send_ref, pieces):
    for side in range(2):
        cols = slice(128 * side, 128 * (side + 1))

        def fill(ref):
            at = 0
            for piece in pieces:
                ref[at : at + piece.shape[0], :] = piece[:, cols]
                at += piece.shape[0]

        @pl.when(place_ref[1] == side)
        def _():
            fill(keep_ref)

        @pl.when(place_ref[1] != side)
        def _():
            fill(send_ref)


def top_kernel(
    place_ref, hid_hbm, slope_hbm, ab_ref, got_ref, rank_ref, w4_ref,
    back_ref, keep_ref, send_ref, hid, slope, front, heads, mid, last, w4h, sems,
):
    steps = hid.shape[0]

    def copies(i):
        return (
            pltpu.make_async_copy(slope_hbm.at[i], slope.at[i], sems.at[0, i]),
            pltpu.make_async_copy(hid_hbm.at[i], hid.at[i], sems.at[1, i]),
        )

    for i in range(steps):
        for copy in copies(i):
            copy.start()

    planes = rank_ref.shape[1]

    def one(v, _):
        mine = rank_ref[v]
        total = jnp.zeros((planes, 128), F32)
        for u in range(NV):
            total += jnp.where(rank_ref[u] < mine, got_ref[u, :planes], 0.0)
        front[v] = jnp.exp(total)
        return 0

    lax.fori_loop(0, NV, one, 0)
    me = place_ref[0]
    mine = rank_ref[me]
    behind = jnp.zeros((planes, 128), F32)
    for u in range(NV):
        behind += jnp.where(rank_ref[u] > mine, front[u] * got_ref[u, planes:], 0.0)
    prefix = front[me]
    rows = heads.reshape(planes * 4 * SAMP, 128)
    for r in range(4 * SAMP):
        value = ab_ref[r] * prefix
        if r < SAMP:
            value = value - ab_ref[16 + r] * behind
        rows[pl.ds(r, planes, stride=4 * SAMP), :] = value
    mid[...] = jnp.zeros_like(mid)
    last[...] = jnp.zeros_like(last)
    pick4 = (group_rows(4 * SAMP, 4).astype(F32) * 0.5).astype(BF16)
    w4h[...] = dot(w4_ref[...], pick4, 0, 1).astype(BF16)
    per = TILE // 128

    def step(i, _):
        for copy in copies(i):
            copy.wait()
        ghead = jnp.concatenate([heads[i * per + k] for k in range(per)], axis=1)
        ghead = spread(ghead.astype(BF16), jnp.zeros((), BF16))
        back = bend(dot(w4h[...], ghead, 1, 0), slope[i])
        back_ref[i] = back
        last[...] += dot(ghead, hid[i, 1], 1, 1)
        mid[...] += dot(hid[i, 0], back, 1, 1)
        return 0

    lax.fori_loop(0, steps, step, 0, unroll=2)
    pick8 = group_rows(4 * SAMP, 8).astype(F32)
    tail = dot(pick8, last[...], 0, 0, lax.Precision.HIGHEST)
    split(place_ref, keep_ref, send_ref, (mid[...], tail))


def middle_kernel(
    place_ref, hid_ref, slope_ref, back_ref, wm_ref, down_ref, keep_ref, send_ref, mid, halved
):
    mid[...] = jnp.zeros_like(mid)
    halved[...] = (wm_ref[1].astype(F32) * 0.5).astype(BF16)

    def step(i, _):
        down = bend(dot(halved[...], back_ref[i], 1, 0), slope_ref[i])
        down_ref[i] = down
        mid[...] += dot(hid_ref[i], down, 1, 1)
        return 0

    lax.fori_loop(0, hid_ref.shape[0], step, 0, unroll=2)
    split(place_ref, keep_ref, send_ref, (mid[...],))


def low_kernel(slope_ref, x_ref, back_ref, wm_ref, out_ref, first, halved):
    first[...] = jnp.zeros_like(first)
    halved[...] = (wm_ref[0].astype(F32) * 0.5).astype(BF16)

    def step(i, _):
        rays = pl.ds(pl.multiple_of(i * TILE, TILE), TILE)
        down = bend(dot(halved[...], back_ref[i], 1, 0), slope_ref[i])
        first[...] += dot(spread(x_ref[:, rays], jnp.zeros((), BF16)), down, 1, 1)
        return 0

    lax.fori_loop(0, slope_ref.shape[0], step, 0, unroll=2)
    pick = group_rows(FEAT * SAMP, FEAT).astype(F32)
    small = dot(pick, first[...], 0, 0, lax.Precision.HIGHEST)
    out_ref[:FEAT] = small[:, :128]
    out_ref[FEAT:] = small[:, 128:]


def unpack_kernel(
    place_ref, a_ref, a_other, b_ref, b_other, first_ref, mid_ref, last_ref
):
    for side in range(2):
        cols = slice(128 * side, 128 * (side + 1))

        rows = slice(256 + FEAT * side, 256 + FEAT * (side + 1))
        first_ref[:, cols] = b_ref[rows, :] + b_other[rows, :]

        def emit(up, down):
            mid_ref[1, :, cols] = up[0:256, :]
            last_ref[:, cols] = up[256:260, :]
            mid_ref[0, :, cols] = down[0:256, :]

        @pl.when(place_ref[1] == side)
        def _():
            emit(a_ref, b_ref)

        @pl.when(place_ref[1] != side)
        def _():
            emit(a_other, b_other)


def far(value):
    return pltpu.with_memory_space_constraint(value, HBM)


def near(value):
    return pltpu.with_memory_space_constraint(value, VMEM)


def forward(x, deltas, counts, cot, w1, wm, w4):
    rays = x.shape[1]
    whole2 = lambda i: (0, 0)
    inside = pl.BlockSpec(memory_space=VMEM)
    return pl.pallas_call(
        forward_kernel,
        grid=(rays // TILE,),
        in_specs=[
            inside,
            pl.BlockSpec((SAMP, rays), whole2),
            pl.BlockSpec((1, rays), whole2),
            pl.BlockSpec((3, rays), whole2),
            pl.BlockSpec((FEAT, W), whole2),
            pl.BlockSpec((2, W, W), lambda i: (0, 0, 0)),
            pl.BlockSpec((4, W), whole2),
        ],
        out_specs=[
            pl.BlockSpec((1, 2, W, SAMP * TILE), lambda i: (i, 0, 0, 0)),
            pl.BlockSpec((1, W, SAMP * TILE), lambda i: (i, 0, 0)),
        ] + [inside] * 4,
        out_shape=[
            pltpu.HBM((rays // TILE, 2, W, SAMP * TILE), BF16),
            pltpu.HBM((rays // TILE, W, SAMP * TILE), BF16),
            pltpu.VMEM((20, rays // 128, 128), F32),
            pltpu.VMEM((NV, 2 * rays // 128, 128), F32),
            pltpu.VMEM((W, FEAT * SAMP), BF16),
            pltpu.VMEM((2, W, W), BF16),
        ],
        scratch_shapes=[
            pltpu.VMEM((4 * SAMP, W), BF16),
            pltpu.VMEM((rays // 128, 4 * SAMP, 128), F32),
            pltpu.VMEM((rays // 128, 8, 128), F32),
        ],
        compiler_params=pltpu.CompilerParams(vmem_limit_bytes=40 * MIB),
        cost_estimate=pl.CostEstimate(
            flops=2 * SAMP * rays * 140288, transcendentals=3 * W * SAMP * rays,
            bytes_accessed=MIB,
        ),
        name="forward",
    )(near(x), far(deltas), far(counts), far(cot), far(w1), far(wm), far(w4))


def slopes(x, low_hid, hid, w1t, wmt):
    steps, _, _, n = hid.shape
    block = pl.BlockSpec((1, W, n), lambda i: (i, 0, 0))
    inside = pl.BlockSpec(memory_space=VMEM)
    return pl.pallas_call(
        slope_kernel,
        grid=(steps,),
        in_specs=[
            inside,
            block,
            pl.BlockSpec((1, 1, W, n), lambda i: (i, 0, 0, 0)),
            inside, inside,
        ],
        out_specs=[block] * 3,
        out_shape=[pltpu.HBM((steps, W, n), BF16)] * 3,
        compiler_params=pltpu.CompilerParams(vmem_limit_bytes=LIMIT),
        cost_estimate=pl.CostEstimate(
            flops=2 * steps * n * 140000, transcendentals=3 * W * steps * n,
            bytes_accessed=20 * MIB,
        ),
        name="slopes",
    )(near(x), far(low_hid), far(hid), near(w1t), near(wmt))


def top(place, hid, slope, ab, got, ranks, w4):
    inside = pl.BlockSpec(memory_space=VMEM)
    steps, _, _, n = hid.shape
    return pl.pallas_call(
        top_kernel,
        in_specs=[pl.BlockSpec(memory_space=SMEM)] + [pl.BlockSpec(memory_space=HBM)] * 2 + [inside] * 4,
        out_specs=[inside] * 3,
        out_shape=[
            pltpu.VMEM((steps, W, n), BF16),
            pltpu.VMEM((264, 128), F32),
            pltpu.VMEM((264, 128), F32),
        ],
        scratch_shapes=[
            pltpu.VMEM(hid.shape, BF16),
            pltpu.VMEM(slope.shape, BF16),
            pltpu.VMEM((NV,) + ab.shape[1:], F32),
            pltpu.VMEM((ab.shape[1], 4 * SAMP, 128), F32),
            pltpu.VMEM((W, W), F32),
            pltpu.VMEM((4 * SAMP, W), F32),
            pltpu.VMEM((W, 4 * SAMP), BF16),
            pltpu.SemaphoreType.DMA((2, steps)),
        ],
        compiler_params=pltpu.CompilerParams(vmem_limit_bytes=24 * MIB),
        cost_estimate=pl.CostEstimate(
            flops=2 * steps * n * 80000, transcendentals=0, bytes_accessed=12 * MIB
        ),
        name="top",
    )(place, far(hid), far(slope), near(ab), near(got), near(ranks), near(w4))


def middle(place, hid, slope, back, wm):
    inside = pl.BlockSpec(memory_space=VMEM)
    steps, _, n = hid.shape
    return pl.pallas_call(
        middle_kernel,
        in_specs=[pl.BlockSpec(memory_space=SMEM)] + [inside] * 4,
        out_specs=[inside] * 3,
        out_shape=[
            pltpu.VMEM((steps, W, n), BF16),
            pltpu.VMEM((256, 128), F32),
            pltpu.VMEM((256, 128), F32),
        ],
        scratch_shapes=[pltpu.VMEM((W, W), F32), pltpu.VMEM((W, W), BF16)],
        compiler_params=pltpu.CompilerParams(vmem_limit_bytes=12 * MIB),
        cost_estimate=pl.CostEstimate(
            flops=2 * steps * n * 131072, transcendentals=0, bytes_accessed=8 * MIB
        ),
        name="middle",
    )(place, near(hid), near(slope), near(back), near(wm))


def low(slope, x, back, wm):
    inside = pl.BlockSpec(memory_space=VMEM)
    steps, _, n = slope.shape
    return pl.pallas_call(
        low_kernel,
        in_specs=[inside] * 4,
        out_specs=inside,
        out_shape=pltpu.VMEM((2 * FEAT, 128), F32),
        scratch_shapes=[pltpu.VMEM((FEAT * SAMP, W), F32), pltpu.VMEM((W, W), BF16)],
        compiler_params=pltpu.CompilerParams(vmem_limit_bytes=12 * MIB),
        cost_estimate=pl.CostEstimate(
            flops=2 * steps * n * 90000, transcendentals=0, bytes_accessed=8 * MIB
        ),
        name="low",
    )(near(slope), near(x), near(back), near(wm))


def unpack(place, *parts):
    inside = pl.BlockSpec(memory_space=VMEM)
    return pl.pallas_call(
        unpack_kernel,
        grid=(1,),
        in_specs=[pl.BlockSpec(memory_space=SMEM)] + [inside] * 4,
        out_specs=[
            pl.BlockSpec((FEAT, W), lambda i: (0, 0)),
            pl.BlockSpec((2, W, W), lambda i: (0, 0, 0)),
            pl.BlockSpec((4, W), lambda i: (0, 0)),
        ],
        out_shape=[
            pltpu.HBM((FEAT, W), F32),
            pltpu.HBM((2, W, W), F32),
            pltpu.HBM((4, W), F32),
        ],
        compiler_params=pltpu.CompilerParams(vmem_limit_bytes=12 * MIB),
        name="unpack",
    )(place, *map(near, parts))


PAIR = [(0, 1), (1, 0)]
NEAR = [(0, 1), (1, 0), (2, 3), (3, 2)]
FAR = [(0, 3), (3, 0), (1, 2), (2, 1)]


def over_cores(keep, send):
    got = lax.ppermute(send, "core", PAIR)
    return keep + got


def over_x(value, ring):
    got = lax.ppermute(value, "x", ring)
    return value + got


def per_device(
    features, deltas, counts, order_rank, cotangent, first_weight, middle_weight, last_weight
):
    x = features[0].reshape(FEAT * SAMP, -1)
    place = jnp.stack([lax.axis_index(("z", "y")), lax.axis_index("core")]).astype(jnp.int32)
    ranks = order_rank.T.reshape(NV, -1, 128)
    w1, wm, w4 = first_weight[0], middle_weight[0], last_weight[0].T
    hid, low_hid, ab, pay, w1t, wmt = forward(x, deltas[0], counts, cotangent, w1, wm, w4)
    got = lax.all_to_all(pay, ("z", "y"), 0, 0, tiled=True)
    low_slope, mid_slope, top_slope = slopes(x, low_hid, hid, w1t, wmt)
    back, *sums = top(place, hid, top_slope, ab, got, ranks, w4)
    upper = over_cores(*sums)
    back, *sums = middle(place, low_hid, mid_slope, back, wm)
    lower = over_cores(*sums)
    small = low(low_slope, x, back, wm)
    lower = jnp.concatenate([lower, small], axis=0)
    upper, lower = over_x(upper, NEAR), over_x(lower, FAR)
    upper, lower = over_x(upper, FAR), over_x(lower, NEAR)
    parts = []
    for part in (upper, lower):
        parts += [part, lax.ppermute(part, "core", PAIR)]
    first, mid, last = unpack(place, *parts)
    return (first[None], mid[None], last.T[None])


def solution(mesh):
    fine = Mesh(mesh.devices.reshape(8, 4, 4, 2), ("z", "y", "x", "core"))
    vol, rep = ("z", "y"), ("x", "core")
    placed = (
        P(vol, None, None, rep),
        P(vol, None, rep),
        P(vol, rep),
        P(rep, None),
        P(None, rep),
        P(vol, None, None),
        P(vol, None, None, None),
        P(vol, None, None),
    )
    return jax.shard_map(
        per_device,
        mesh=fine,
        in_specs=placed,
        out_specs=(P(vol, None, None), P(vol, None, None, None), P(vol, None, None)),
        check_vma=False,
    )
```

```python
import jax
import jax.numpy as jnp
from jax import lax
from jax.experimental import pallas as pl
from jax.experimental.pallas import tpu as pltpu
from jax.sharding import Mesh, PartitionSpec as P


F32 = jnp.float32
BF16 = jnp.bfloat16
TILE = 512
PART = 256
SAMP = 4
FEAT = 32
W = 256
NV = 32
MIB = 1024 * 1024
HBM = pltpu.MemorySpace.HBM
VMEM = pltpu.MemorySpace.VMEM
SMEM = pltpu.MemorySpace.SMEM
LIMIT = 24 * MIB


def dot(lhs, rhs, lhs_dim, rhs_dim, precision=None):
    return lax.dot_general(
        lhs, rhs, (((lhs_dim,), (rhs_dim,)), ((), ())),
        preferred_element_type=F32, precision=precision,
    )


def group_rows(rows, width):
    i = lax.broadcasted_iota(jnp.int32, (rows, width), 0)
    j = lax.broadcasted_iota(jnp.int32, (rows, width), 1)
    return lax.shift_right_logical(i, 2) == j


def spread(block, fill):
    row = lax.broadcasted_iota(jnp.int32, block.shape, 0)
    parts = [jnp.where((row & 3) == s, block, fill) for s in range(SAMP)]
    return jnp.concatenate(parts, axis=1)


def by_row(ref, row):
    planes, rows, _ = ref.shape
    return ref.reshape(planes * rows, 128)[pl.ds(row, planes, stride=rows), :]


def forward_kernel(
    x_ref, delta_ref, count_ref, cot_ref, w1_ref, wm_ref, w4_ref,
    hid_ref, low_ref, ab_ref, pay_ref, w1t, wmt, w4t, heads, given,
):
    step = pl.program_id(0)
    tile = TILE

    @pl.when(step == 0)
    def _():
        pick = group_rows(FEAT * SAMP, FEAT).astype(BF16)
        w1t[...] = (dot(w1_ref[...], pick, 0, 1) * 0.5).astype(BF16)
        for k in range(2):
            wmt[k] = (wm_ref[k].astype(F32).T * 0.5).astype(BF16)
        pick4 = group_rows(4 * SAMP, 4).astype(BF16)
        w4t[...] = dot(pick4, w4_ref[...], 1, 0).astype(BF16)
        for r in range(given.shape[0]):
            lanes = slice(128 * r, 128 * (r + 1))
            given[r, 0:4, :] = delta_ref[:, lanes]
            given[r, 4:5, :] = count_ref[:, lanes].astype(F32)
            given[r, 5:8, :] = cot_ref[:, lanes]

    row16 = lax.broadcasted_iota(jnp.int32, (4 * SAMP, W), 0) & 3
    parts = range(tile // PART)
    halves = []
    for part in parts:
        rays = pl.ds(pl.multiple_of(step * tile + part * PART, PART), PART)
        halves.append(dot(w1t[...], spread(x_ref[:, rays], jnp.zeros((), BF16)), 1, 0))
    for k in range(3):
        hiddens = []
        for part in parts:
            half = halves[part]
            hidden = (half + half * jnp.tanh(half)).astype(BF16)
            hiddens.append(hidden)
            for s in range(SAMP):
                cols = slice(s * PART, (s + 1) * PART)
                put = slice(s * tile + part * PART, s * tile + (part + 1) * PART)
                if k == 0:
                    low_ref[0, :, put] = hidden[:, cols]
                else:
                    hid_ref[0, k - 1, :, put] = hidden[:, cols]
            if k < 2:
                halves[part] = dot(wmt[k], hidden, 1, 0)
    for part in parts:
        head = jnp.zeros((4 * SAMP, PART), F32)
        for s in range(SAMP):
            head += dot(
                jnp.where(row16 == s, w4t[...], jnp.zeros((), BF16)),
                hiddens[part][:, s * PART : (s + 1) * PART], 1, 0,
            )
        for r in range(PART // 128):
            heads[step * (tile // 128) + part * (PART // 128) + r] = head[:, 128 * r : 128 * (r + 1)]

    @pl.when(step == pl.num_programs(0) - 1)
    def _():
        render(heads, given, ab_ref, pay_ref)


def render(heads, given, ab_ref, pay_ref):
    planes = heads.shape[0]
    zero = jnp.zeros((planes, 128), F32)
    counts = by_row(given, 4)
    cot = [by_row(given, 5 + c) for c in range(3)]
    reached, leaving = zero, jnp.ones((planes, 128), F32)
    share, left, facing, own = [], [], [], []
    for s in range(SAMP):
        raw = by_row(heads, s)
        density = jnp.maximum(raw, 0.0) + jnp.log1p(jnp.exp(-jnp.abs(raw)))
        span = jnp.where(counts > s, by_row(given, s), 0.0)
        reached = reached + density * span
        entering, leaving = leaving, jnp.exp(-reached)
        share.append(entering - leaving)
        left.append(leaving)
        own.append(span * jax.nn.sigmoid(raw))
        total = zero
        for c in range(3):
            albedo = jax.nn.sigmoid(by_row(heads, 4 * (c + 1) + s))
            lit = cot[c] * albedo
            total = total + lit
            ab_ref[4 * (c + 1) + s] = share[s] * lit * (1.0 - albedo)
        facing.append(total)
    later = zero
    for s in reversed(range(SAMP)):
        ab_ref[s] = (facing[s] * left[s] - later) * own[s]
        ab_ref[16 + s] = own[s]
        later = later + facing[s] * share[s]
    both = jnp.concatenate([-reached, later], axis=0)
    pay_ref[...] = jnp.broadcast_to(both[None], pay_ref.shape)


def slope_kernel(x_ref, low_hid, mid_hid, w1t, wmt, low_ref, mid_ref, top_ref):
    i = pl.program_id(0)
    x = x_ref[:, pl.ds(pl.multiple_of(i * TILE, TILE), TILE)]
    row = lax.broadcasted_iota(jnp.int32, x.shape, 0) & 3
    for s in range(SAMP):
        cols = slice(s * TILE, (s + 1) * TILE)
        wide = jnp.where(row == s, x, jnp.zeros((), BF16))
        for ref, weight, taken in (
            (low_ref, w1t[...], wide),
            (mid_ref, wmt[0], low_hid[0, :, cols]),
            (top_ref, wmt[1], mid_hid[0, 0, :, cols]),
        ):
            half = dot(weight, taken, 1, 0)
            curve = jnp.tanh(half)
            ref[0, :, cols] = (half + curve * (1.0 - half * curve)).astype(BF16)


def bend(back, slope):
    return (back + back * slope.astype(F32)).astype(BF16)


def split(place_ref, keep_ref, send_ref, pieces):
    for side in range(2):
        cols = slice(128 * side, 128 * (side + 1))

        def fill(ref):
            at = 0
            for piece in pieces:
                ref[at : at + piece.shape[0], :] = piece[:, cols]
                at += piece.shape[0]

        @pl.when(place_ref[1] == side)
        def _():
            fill(keep_ref)

        @pl.when(place_ref[1] != side)
        def _():
            fill(send_ref)


def top_kernel(
    place_ref, hid_hbm, slope_hbm, ab_ref, got_ref, rank_ref, w4_ref,
    back_ref, keep_ref, send_ref, hid, slope, front, heads, mid, last, w4h, sems,
):
    steps = hid.shape[0]

    def copies(i):
        return (
            pltpu.make_async_copy(slope_hbm.at[i], slope.at[i], sems.at[0, i]),
            pltpu.make_async_copy(hid_hbm.at[i], hid.at[i], sems.at[1, i]),
        )

    for i in range(steps):
        for copy in copies(i):
            copy.start()

    planes = rank_ref.shape[1]

    def one(v, _):
        mine = rank_ref[v]
        total = jnp.zeros((planes, 128), F32)
        for u in range(NV):
            total += jnp.where(rank_ref[u] < mine, got_ref[u, :planes], 0.0)
        front[v] = jnp.exp(total)
        return 0

    lax.fori_loop(0, NV, one, 0, unroll=4)
    me = place_ref[0]
    mine = rank_ref[me]
    behind = jnp.zeros((planes, 128), F32)
    for u in range(NV):
        behind += jnp.where(rank_ref[u] > mine, front[u] * got_ref[u, planes:], 0.0)
    prefix = front[me]
    rows = heads.reshape(planes * 4 * SAMP, 128)
    for r in range(4 * SAMP):
        value = ab_ref[r] * prefix
        if r < SAMP:
            value = value - ab_ref[16 + r] * behind
        rows[pl.ds(r, planes, stride=4 * SAMP), :] = value
    mid[...] = jnp.zeros_like(mid)
    last[...] = jnp.zeros_like(last)
    pick4 = (group_rows(4 * SAMP, 4).astype(F32) * 0.5).astype(BF16)
    w4h[...] = dot(w4_ref[...], pick4, 0, 1).astype(BF16)
    per = TILE // 128

    def step(i, _):
        for copy in copies(i):
            copy.wait()
        ghead = jnp.concatenate([heads[i * per + k] for k in range(per)], axis=1)
        ghead = spread(ghead.astype(BF16), jnp.zeros((), BF16))
        back = bend(dot(w4h[...], ghead, 1, 0), slope[i])
        back_ref[i] = back
        last[...] += dot(ghead, hid[i, 1], 1, 1)
        mid[...] += dot(hid[i, 0], back, 1, 1)
        return 0

    lax.fori_loop(0, steps, step, 0, unroll=2)
    pick8 = group_rows(4 * SAMP, 8).astype(F32)
    tail = dot(pick8, last[...], 0, 0, lax.Precision.HIGHEST)
    split(place_ref, keep_ref, send_ref, (mid[...], tail))


def middle_kernel(
    place_ref, hid_ref, slope_ref, back_ref, wm_ref, down_ref, keep_ref, send_ref, mid, halved
):
    mid[...] = jnp.zeros_like(mid)
    halved[...] = (wm_ref[1].astype(F32) * 0.5).astype(BF16)

    def step(i, _):
        down = bend(dot(halved[...], back_ref[i], 1, 0), slope_ref[i])
        down_ref[i] = down
        mid[...] += dot(hid_ref[i], down, 1, 1)
        return 0

    lax.fori_loop(0, hid_ref.shape[0], step, 0, unroll=4)
    split(place_ref, keep_ref, send_ref, (mid[...],))


def low_kernel(slope_ref, x_ref, back_ref, wm_ref, out_ref, first, halved):
    first[...] = jnp.zeros_like(first)
    halved[...] = (wm_ref[0].astype(F32) * 0.5).astype(BF16)

    def step(i, _):
        rays = pl.ds(pl.multiple_of(i * TILE, TILE), TILE)
        down = bend(dot(halved[...], back_ref[i], 1, 0), slope_ref[i])
        first[...] += dot(spread(x_ref[:, rays], jnp.zeros((), BF16)), down, 1, 1)
        return 0

    lax.fori_loop(0, slope_ref.shape[0], step, 0, unroll=4)
    pick = group_rows(FEAT * SAMP, FEAT).astype(F32)
    small = dot(pick, first[...], 0, 0, lax.Precision.HIGHEST)
    out_ref[:FEAT] = small[:, :128]
    out_ref[FEAT:] = small[:, 128:]


def unpack_kernel(
    place_ref, a_ref, a_other, b_ref, b_other, first_ref, mid_ref, last_ref
):
    for side in range(2):
        cols = slice(128 * side, 128 * (side + 1))

        rows = slice(256 + FEAT * side, 256 + FEAT * (side + 1))
        first_ref[:, cols] = b_ref[rows, :] + b_other[rows, :]

        def emit(up, down):
            mid_ref[1, :, cols] = up[0:256, :]
            last_ref[:, cols] = up[256:260, :]
            mid_ref[0, :, cols] = down[0:256, :]

        @pl.when(place_ref[1] == side)
        def _():
            emit(a_ref, b_ref)

        @pl.when(place_ref[1] != side)
        def _():
            emit(a_other, b_other)


def far(value):
    return pltpu.with_memory_space_constraint(value, HBM)


def near(value):
    return pltpu.with_memory_space_constraint(value, VMEM)


def forward(x, deltas, counts, cot, w1, wm, w4):
    rays = x.shape[1]
    whole2 = lambda i: (0, 0)
    inside = pl.BlockSpec(memory_space=VMEM)
    return pl.pallas_call(
        forward_kernel,
        grid=(rays // TILE,),
        in_specs=[
            inside,
            pl.BlockSpec((SAMP, rays), whole2),
            pl.BlockSpec((1, rays), whole2),
            pl.BlockSpec((3, rays), whole2),
            pl.BlockSpec((FEAT, W), whole2),
            pl.BlockSpec((2, W, W), lambda i: (0, 0, 0)),
            pl.BlockSpec((4, W), whole2),
        ],
        out_specs=[
            pl.BlockSpec((1, 2, W, SAMP * TILE), lambda i: (i, 0, 0, 0)),
            pl.BlockSpec((1, W, SAMP * TILE), lambda i: (i, 0, 0)),
        ] + [inside] * 4,
        out_shape=[
            pltpu.HBM((rays // TILE, 2, W, SAMP * TILE), BF16),
            pltpu.HBM((rays // TILE, W, SAMP * TILE), BF16),
            pltpu.VMEM((20, rays // 128, 128), F32),
            pltpu.VMEM((NV, 2 * rays // 128, 128), F32),
            pltpu.VMEM((W, FEAT * SAMP), BF16),
            pltpu.VMEM((2, W, W), BF16),
        ],
        scratch_shapes=[
            pltpu.VMEM((4 * SAMP, W), BF16),
            pltpu.VMEM((rays // 128, 4 * SAMP, 128), F32),
            pltpu.VMEM((rays // 128, 8, 128), F32),
        ],
        compiler_params=pltpu.CompilerParams(vmem_limit_bytes=40 * MIB),
        cost_estimate=pl.CostEstimate(
            flops=2 * SAMP * rays * 140288, transcendentals=3 * W * SAMP * rays,
            bytes_accessed=MIB,
        ),
        name="forward",
    )(near(x), far(deltas), far(counts), far(cot), far(w1), far(wm), far(w4))


def slopes(x, low_hid, hid, w1t, wmt):
    steps, _, _, n = hid.shape
    block = pl.BlockSpec((1, W, n), lambda i: (i, 0, 0))
    inside = pl.BlockSpec(memory_space=VMEM)
    return pl.pallas_call(
        slope_kernel,
        grid=(steps,),
        in_specs=[
            inside,
            block,
            pl.BlockSpec((1, 1, W, n), lambda i: (i, 0, 0, 0)),
            inside, inside,
        ],
        out_specs=[block] * 3,
        out_shape=[pltpu.HBM((steps, W, n), BF16)] * 3,
        compiler_params=pltpu.CompilerParams(vmem_limit_bytes=LIMIT),
        cost_estimate=pl.CostEstimate(
            flops=2 * steps * n * 140000, transcendentals=3 * W * steps * n,
            bytes_accessed=20 * MIB,
        ),
        name="slopes",
    )(near(x), far(low_hid), far(hid), near(w1t), near(wmt))


def top(place, hid, slope, ab, got, ranks, w4):
    inside = pl.BlockSpec(memory_space=VMEM)
    steps, _, _, n = hid.shape
    return pl.pallas_call(
        top_kernel,
        in_specs=[pl.BlockSpec(memory_space=SMEM)] + [pl.BlockSpec(memory_space=HBM)] * 2 + [inside] * 4,
        out_specs=[inside] * 3,
        out_shape=[
            pltpu.VMEM((steps, W, n), BF16),
            pltpu.VMEM((264, 128), F32),
            pltpu.VMEM((264, 128), F32),
        ],
        scratch_shapes=[
            pltpu.VMEM(hid.shape, BF16),
            pltpu.VMEM(slope.shape, BF16),
            pltpu.VMEM((NV,) + ab.shape[1:], F32),
            pltpu.VMEM((ab.shape[1], 4 * SAMP, 128), F32),
            pltpu.VMEM((W, W), F32),
            pltpu.VMEM((4 * SAMP, W), F32),
            pltpu.VMEM((W, 4 * SAMP), BF16),
            pltpu.SemaphoreType.DMA((2, steps)),
        ],
        compiler_params=pltpu.CompilerParams(vmem_limit_bytes=24 * MIB),
        cost_estimate=pl.CostEstimate(
            flops=2 * steps * n * 80000, transcendentals=0, bytes_accessed=12 * MIB
        ),
        name="top",
    )(place, far(hid), far(slope), near(ab), near(got), near(ranks), near(w4))


def middle(place, hid, slope, back, wm):
    inside = pl.BlockSpec(memory_space=VMEM)
    steps, _, n = hid.shape
    return pl.pallas_call(
        middle_kernel,
        in_specs=[pl.BlockSpec(memory_space=SMEM)] + [inside] * 4,
        out_specs=[inside] * 3,
        out_shape=[
            pltpu.VMEM((steps, W, n), BF16),
            pltpu.VMEM((256, 128), F32),
            pltpu.VMEM((256, 128), F32),
        ],
        scratch_shapes=[pltpu.VMEM((W, W), F32), pltpu.VMEM((W, W), BF16)],
        compiler_params=pltpu.CompilerParams(vmem_limit_bytes=12 * MIB),
        cost_estimate=pl.CostEstimate(
            flops=2 * steps * n * 131072, transcendentals=0, bytes_accessed=8 * MIB
        ),
        name="middle",
    )(place, near(hid), near(slope), near(back), near(wm))


def low(slope, x, back, wm):
    inside = pl.BlockSpec(memory_space=VMEM)
    steps, _, n = slope.shape
    return pl.pallas_call(
        low_kernel,
        in_specs=[inside] * 4,
        out_specs=inside,
        out_shape=pltpu.VMEM((2 * FEAT, 128), F32),
        scratch_shapes=[pltpu.VMEM((FEAT * SAMP, W), F32), pltpu.VMEM((W, W), BF16)],
        compiler_params=pltpu.CompilerParams(vmem_limit_bytes=12 * MIB),
        cost_estimate=pl.CostEstimate(
            flops=2 * steps * n * 90000, transcendentals=0, bytes_accessed=8 * MIB
        ),
        name="low",
    )(near(slope), near(x), near(back), near(wm))


def unpack(place, *parts):
    inside = pl.BlockSpec(memory_space=VMEM)
    return pl.pallas_call(
        unpack_kernel,
        grid=(1,),
        in_specs=[pl.BlockSpec(memory_space=SMEM)] + [inside] * 4,
        out_specs=[
            pl.BlockSpec((FEAT, W), lambda i: (0, 0)),
            pl.BlockSpec((2, W, W), lambda i: (0, 0, 0)),
            pl.BlockSpec((4, W), lambda i: (0, 0)),
        ],
        out_shape=[
            pltpu.HBM((FEAT, W), F32),
            pltpu.HBM((2, W, W), F32),
            pltpu.HBM((4, W), F32),
        ],
        compiler_params=pltpu.CompilerParams(vmem_limit_bytes=12 * MIB),
        name="unpack",
    )(place, *map(near, parts))


PAIR = [(0, 1), (1, 0)]
NEAR = [(0, 1), (1, 0), (2, 3), (3, 2)]
FAR = [(0, 3), (3, 0), (1, 2), (2, 1)]


def over_cores(keep, send):
    got = lax.ppermute(send, "core", PAIR)
    return keep + got


def over_x(value, ring):
    got = lax.ppermute(value, "x", ring)
    return value + got


def per_device(
    features, deltas, counts, order_rank, cotangent, first_weight, middle_weight, last_weight
):
    x = features[0].reshape(FEAT * SAMP, -1)
    place = jnp.stack([lax.axis_index(("z", "y")), lax.axis_index("core")]).astype(jnp.int32)
    ranks = order_rank.T.reshape(NV, -1, 128)
    w1, wm, w4 = first_weight[0], middle_weight[0], last_weight[0].T
    hid, low_hid, ab, pay, w1t, wmt = forward(x, deltas[0], counts, cotangent, w1, wm, w4)
    got = lax.all_to_all(pay, ("z", "y"), 0, 0, tiled=True)
    low_slope, mid_slope, top_slope = slopes(x, low_hid, hid, w1t, wmt)
    back, *sums = top(place, hid, top_slope, ab, got, ranks, w4)
    upper = over_cores(*sums)
    back, *sums = middle(place, low_hid, mid_slope, back, wm)
    lower = over_cores(*sums)
    small = low(low_slope, x, back, wm)
    lower = jnp.concatenate([lower, small], axis=0)
    upper, lower = over_x(upper, NEAR), over_x(lower, FAR)
    upper, lower = over_x(upper, FAR), over_x(lower, NEAR)
    parts = []
    for part in (upper, lower):
        parts += [part, lax.ppermute(part, "core", PAIR)]
    first, mid, last = unpack(place, *parts)
    return (first[None], mid[None], last.T[None])


def solution(mesh):
    fine = Mesh(mesh.devices.reshape(8, 4, 4, 2), ("z", "y", "x", "core"))
    vol, rep = ("z", "y"), ("x", "core")
    placed = (
        P(vol, None, None, rep),
        P(vol, None, rep),
        P(vol, rep),
        P(rep, None),
        P(None, rep),
        P(vol, None, None),
        P(vol, None, None, None),
        P(vol, None, None),
    )
    return jax.shard_map(
        per_device,
        mesh=fine,
        in_specs=placed,
        out_specs=(P(vol, None, None), P(vol, None, None, None), P(vol, None, None)),
        check_vma=False,
    )
```
